256 devices in a mesh: gx: 8 (over x, core), gy: 32 (over y, z).
Axes of the slice: x: 4, y: 4, z: 8, core: 2. Of those that a mesh axis runs over, the one named last changes fastest.
Arguments:
- state: float32 [5, 16, 1024, 2048], P(None, None, 'gy', 'gx'), may hold values from -5 to 5
- increment: float32 [5, 16, 1024, 2048], P(None, None, 'gy', 'gx'), may hold values from -6 to 6
- jacobian: float32 [5, 5, 1024], P(None, None, 'gy'), may hold values from -2.5 to 2.5
- filter_alpha: float32 [1024], P('gy'), may hold values from 0.49996 to 0.499996
- filter_beta: float32 [1024], P('gy'), may hold values from 1e-06 to 1.5e-05
Outputs:
- new_state: float32 [5, 16, 1024, 2048], P(None, None, 'gy', 'gx')
- new_increment: float32 [5, 16, 1024, 2048], P(None, None, 'gy', 'gx')
The draws below stay inside these ranges and needn't reach their ends.
All inputs are finite; a program needn't handle non-finite values.
Results may differ from the reference program's by a relative error of at most 0.0012.
Values sent between devices are 32-bit elements; how exact they have to be, the bound alone decides.
A program may use at most 128 MiB of HBM per device.

```python
import jax
import jax.numpy as jnp
from jax import lax

FIELDS = 5
NY = 1024
Z = 16
NX = 2048


def draw_state(key, part):
    normal_part = jnp.clip(jax.random.normal(key, (FIELDS, Z, NY, NX), jnp.float32), -5.0, 5.0)
    return normal_part


def block_scale(key, dims, shards, low, top_value):
    loudness, own = 1.0, jax.random.fold_in(key, 6)
    for dim, shards_of in shards:
        steps = jnp.exp(jax.random.uniform(jax.random.fold_in(own, dim), (shards_of,), jnp.float32, low / len(shards), top_value / len(shards)))
        loudness = loudness * jnp.repeat(steps, dims[dim] // shards_of).reshape([-1 if axis == dim else 1 for axis in range(len(dims))])
    return loudness


def bell_draw(stream_key, dims, width, most, pieces=(), kind=jnp.bfloat16):
    result = width * jax.random.normal(stream_key, dims, jnp.float32)
    if pieces:
        result = result * block_scale(stream_key, dims, pieces, -0.22, 0.18)
    return jnp.clip(result, -most, most).astype(kind)


def setup_inputs(seed: int = 0) -> dict:
    key_of = jax.random.split(jax.random.key(seed), 6)
    return {
        "state": draw_state(jax.random.fold_in(key_of[5], 71), 0),
        "increment": bell_draw(key_of[1], (FIELDS, Z, NY, NX), 1.0, 6.0, ((2, 32), (3, 8)), jnp.float32),
        "jacobian": bell_draw(key_of[2], (FIELDS, FIELDS, NY), FIELDS ** -0.5, 2.5, ((2, 32),), jnp.float32),
        "filter_alpha": jnp.clip(0.49996 + 3.600120544433594e-05 * jax.random.uniform(key_of[3], (NY,), jnp.float32) ** block_scale(key_of[3], (NY,), ((0, 32),), -0.2, 0.2), 0.49996, 0.499996),
        "filter_beta": jnp.clip(9.999999974752427e-07 + 1.3999999623592885e-05 * jax.random.uniform(key_of[4], (NY,), jnp.float32) ** block_scale(key_of[4], (NY,), ((0, 32),), -0.2, 0.2), 9.999999974752427e-07, 1.4999999621068127e-05),
    }


section_a = -5.0 / 9.0
section_b = 15.0 / 16.0
courant = 0.5

def reference(state, increment, jacobian, filter_alpha, filter_beta):

    def moved(shift_by):
        return jnp.roll(state, -shift_by, axis=3)
    gradient = (45.0 * (moved(1) - moved(-1)) - 9.0 * (moved(2) - moved(-2)) + (moved(3) - moved(-3))) / 60.0
    flux_term = jnp.einsum('fgy,gzyx->fzyx', jacobian, gradient, precision=lax.Precision.HIGHEST)
    new_increment = section_a * increment - courant * flux_term
    source = state + section_b * new_increment
    coef_zero = (5.0 + 6.0 * filter_alpha - 6.0 * filter_beta) / 8.0
    coef_one = (1.0 + 2.0 * filter_alpha + 2.0 * filter_beta) / 2.0
    coef_two = -(1.0 - 2.0 * filter_alpha - 14.0 * filter_beta) / 8.0
    positions = jnp.arange(NY)
    distance = jnp.abs(positions[:, None] - positions[None, :])
    matrix = (distance == 0).astype(filter_alpha.dtype) + filter_alpha[:, None] * (distance == 1).astype(filter_alpha.dtype) + filter_beta[:, None] * (distance == 2).astype(filter_alpha.dtype)

    def solve_field(one_field):
        padded = jnp.pad(one_field, ((0, 0), (2, 2), (0, 0)))
        filter_rhs = coef_zero[None, :, None] * one_field + 0.5 * coef_one[None, :, None] * (padded[:, 3:NY + 3] + padded[:, 1:NY + 1]) + 0.5 * coef_two[None, :, None] * (padded[:, 4:NY + 4] + padded[:, 0:NY])
        right_side = jnp.transpose(filter_rhs, (1, 0, 2)).reshape(NY, Z * NX)
        solved = jnp.linalg.solve(matrix, right_side)
        return jnp.transpose(solved.reshape(NY, Z, NX), (1, 0, 2))
    new_state = lax.map(solve_field, source)
    return (new_state, new_increment)
```

```python
import functools

import jax
import jax.numpy as jnp
from jax import lax
from jax.experimental import pallas as pl
from jax.experimental.pallas import tpu as pltpu
from jax.sharding import PartitionSpec as P

section_a = -5.0 / 9.0
section_b = 15.0 / 16.0
courant = 0.5
MESH = pl.DeviceIdType.MESH
F32 = jnp.float32
BF16 = jnp.bfloat16
FIELDS = 5
ROWS = 32
COLS = 256


def iota(shape, dim):
    return lax.broadcasted_iota(jnp.int32, shape, dim)


def split(x):
    high = x.astype(BF16)
    return high, (x - high.astype(F32)).astype(BF16)


def stencil_weights(rows, offset):
    gap = iota((rows, COLS), 0) + offset - iota((rows, COLS), 1)
    size = jnp.abs(gap)
    weight = jnp.where(size == 1, 45.0, jnp.where(size == 2, -9.0, jnp.where(size == 3, 1.0, 0.0)))
    return jnp.where(gap < 0, -weight, weight)


def before(x, lanes):
    rolled = pltpu.roll(x, 1, 0)
    return jnp.where(iota(x.shape, 0) == 0, pltpu.roll(rolled, 1, 1), rolled)


def after(x, lanes):
    rolled = pltpu.roll(x, ROWS - 1, 0)
    return jnp.where(iota(x.shape, 0) == ROWS - 1, pltpu.roll(rolled, lanes - 1, 1), rolled)


def factors(alpha, beta, blocks):
    shape = alpha.shape
    lanes = shape[1]
    point = iota(shape, 0) + ROWS * iota(shape, 1)
    last = ROWS * blocks - 1
    inner = (point >= 1) & (point < last)
    low_one = jnp.where((point >= 1) & (point <= last), alpha, 0.0)
    up_one = jnp.where(point < last, alpha, 0.0)
    low_two = jnp.where(inner, after(beta, lanes), 0.0)
    up_two = jnp.where(inner, before(beta, lanes), 0.0)
    a, e, b = low_one, up_one, jnp.ones(shape, F32)
    for _ in range(3):
        l = low_two / jnp.where(inner, after(a, lanes), 1.0)
        u = up_two / jnp.where(inner, before(e, lanes), 1.0)
        a = low_one - b * l
        e = up_one - b * u
        b = (
            1.0
            - a * jnp.where(point >= 1, before(u, lanes), 0.0)
            - e * jnp.where(point < last, after(l, lanes), 0.0)
        )
    return a, b, e, l, u


def kernel(
    blocks,
    planes,
    widths,
    state,
    increment,
    coef_ref,
    jac_ref,
    new_state,
    new_inc,
    st,
    inc,
    gr,
    sx,
    zl,
    jb,
    dxw,
    hxw,
    xl,
    xr,
    hl,
    hr,
    ytop_s,
    ybot_s,
    ytop,
    ybot,
    cb,
    sq,
    tab,
    rows_a,
    rows_b,
    pqs,
    rbuf,
    ss,
    sbuf,
    wmat,
    st_sem,
    inc_sem,
    ns_sem,
    ni_sem,
    loc_sem,
    x_send,
    x_recv,
    c_send,
    c_recv,
    yt_send,
    yt_recv,
    yb_send,
    yb_recv,
    p_send,
    p_recv,
    s_send,
    s_recv,
):
    gx = lax.axis_index("gx")
    me = lax.axis_index("gy")
    left = lax.rem(gx + widths - 1, widths)
    right = lax.rem(gx + 1, widths)
    groups = planes // 4
    home = me // 2
    side = lax.rem(me, 2)

    barrier = pltpu.get_barrier_semaphore()
    pl.semaphore_signal(barrier, inc=1, device_id=(left, me), device_id_type=MESH)
    pl.semaphore_signal(barrier, inc=1, device_id=(right, me), device_id_type=MESH)

    @pl.loop(1, blocks)
    def _(step):
        peer = lax.rem(me + step, blocks)
        pl.semaphore_signal(barrier, inc=1, device_id=(gx, peer), device_id_type=MESH)

    def plane_of(step):
        return lax.rem(step + home, planes)

    def state_in(z):
        return pltpu.make_async_copy(state.at[:, z], st.at[z], st_sem.at[z])

    def inc_in(z):
        return pltpu.make_async_copy(increment.at[:, z], inc.at[z], inc_sem.at[z])

    @pl.loop(0, planes)
    def _(z):
        state_in(z).start()

    @pl.loop(0, planes)
    def _(step):
        inc_in(plane_of(step)).start()

    dxw[...] = stencil_weights(COLS, 0).astype(BF16)
    halo_row = iota((128, COLS), 0)
    hxw[...] = jnp.where(
        halo_row < 3,
        stencil_weights(128, -3),
        jnp.where(halo_row < 6, stencil_weights(128, COLS - 3), 0.0),
    ).astype(BF16)
    sq[...] = jnp.zeros((128, 128), F32)
    sq[0 : FIELDS * FIELDS, 0:ROWS] = jac_ref[...]
    jac_t = sq[...].T
    for fg in range(FIELDS * FIELDS):
        jb[fg] = jnp.broadcast_to(jac_t[0:ROWS, fg : fg + 1], (ROWS, 128)) * (courant / 60.0)

    lane = iota((ROWS, 128), 1)

    @pl.loop(0, groups)
    def _(g):
        to_left = jnp.zeros((ROWS, 128), F32)
        to_right = jnp.zeros((ROWS, 128), F32)
        for q in range(4):
            z = g * 4 + q
            state_in(z).wait()
            for f in range(FIELDS):
                base = q * 32 + f * 6
                first = pltpu.roll(st[z, f, :, 0:128], base + 3, 1)
                final = pltpu.roll(st[z, f, :, 128:256], (base - 125) % 128, 1)
                to_left = jnp.where((lane >= base + 3) & (lane < base + 6), first, to_left)
                to_right = jnp.where((lane >= base) & (lane < base + 3), final, to_right)
        xl[g] = to_left
        xr[g] = to_right

    pl.semaphore_wait(barrier, blocks + 1)

    send_left = pltpu.make_async_remote_copy(
        xl, hr, x_send.at[0], x_recv.at[0], device_id=(left, me), device_id_type=MESH
    )
    send_right = pltpu.make_async_remote_copy(
        xr, hl, x_send.at[1], x_recv.at[1], device_id=(right, me), device_id_type=MESH
    )
    send_left.start()
    send_right.start()

    def coef_out(step):
        peer = lax.rem(me + step, blocks)
        return pltpu.make_async_remote_copy(
            coef_ref,
            cb.at[me],
            c_send.at[step],
            c_recv.at[me],
            device_id=(gx, peer),
            device_id_type=MESH,
        )

    def coef_arrival(k):
        return pltpu.make_async_remote_copy(
            coef_ref,
            cb.at[k],
            c_send.at[0],
            c_recv.at[k],
            device_id=(gx, me),
            device_id_type=MESH,
        )

    @pl.loop(1, blocks)
    def _(step):
        coef_out(step).start()

    cb[me] = coef_ref[...]

    @pl.loop(0, planes)
    def _(z):
        high, low = split(st[z].reshape(FIELDS * ROWS, COLS))
        weights = dxw[...]
        total = jnp.dot(high, weights, preferred_element_type=F32) + jnp.dot(
            low, weights, preferred_element_type=F32
        )
        gr[z] = total.reshape(FIELDS, ROWS, COLS)

    send_left.wait()
    send_right.wait()

    def top_out(z):
        return pltpu.make_async_remote_copy(
            ytop_s.at[z],
            ytop.at[z],
            yt_send.at[z],
            yt_recv.at[z],
            device_id=(gx, lax.rem(me + 1, blocks)),
            device_id_type=MESH,
        )

    def bottom_out(z):
        return pltpu.make_async_remote_copy(
            ybot_s.at[z],
            ybot.at[z],
            yb_send.at[z],
            yb_recv.at[z],
            device_id=(gx, lax.rem(me + blocks - 1, blocks)),
            device_id_type=MESH,
        )

    @pl.loop(0, planes)
    def _(step):
        z = plane_of(step)
        inc_in(z).wait()
        g = z // 4
        halo = hl[g] + hr[g]
        shift = lax.rem(z, 4) * 32
        pieces = [
            pltpu.roll(halo, lax.rem(256 - shift - 6 * f, 128), 1) for f in range(FIELDS)
        ]
        high, low = split(jnp.concatenate(pieces, axis=0))
        weights = hxw[...]
        edge = jnp.dot(high, weights, preferred_element_type=F32) + jnp.dot(
            low, weights, preferred_element_type=F32
        )
        edge = edge.reshape(FIELDS, ROWS, COLS)
        for h in range(2):
            cols = slice(128 * h, 128 * h + 128)
            grads = [gr[z, f, :, cols] + edge[f, :, cols] for f in range(FIELDS)]
            for f in range(FIELDS):
                flux = jb[f * FIELDS] * grads[0]
                for other in range(1, FIELDS):
                    flux = flux + jb[f * FIELDS + other] * grads[other]
                fresh = section_a * inc[z, f, :, cols] - flux
                source = st[z, f, :, cols] + section_b * fresh
                inc[z, f, :, cols] = fresh
                sx[z, f, :, cols] = source
                ybot_s[z, f, :, cols] = source[0:2]
                ytop_s[z, f, :, cols] = source[ROWS - 2 : ROWS]
        pltpu.make_async_copy(inc.at[z], new_inc.at[:, z], ni_sem.at[z]).start()

        @pl.when(me < blocks - 1)
        def _():
            top_out(z).start()

        @pl.when(me > 0)
        def _():
            bottom_out(z).start()

    @pl.loop(1, blocks)
    def _(step):
        coef_arrival(lax.rem(me + blocks - step, blocks)).wait_recv()

    sq[...] = jnp.zeros((128, 128), F32)
    for k in range(blocks):
        sq[k : k + 1, :] = cb[k]
    turned = sq[...].T
    alpha = turned[0:ROWS]
    beta = turned[ROWS : 2 * ROWS]
    a, b, e, l, u = factors(alpha, beta, blocks)
    weight = (1.0 - 2.0 * alpha + 2.0 * beta) * (1.0 / 16.0)
    block_lane = iota((ROWS, 128), 1)
    over_e = -1.0 / jnp.where(e == 0.0, 1.0, e)
    over_a = -1.0 / jnp.where(a == 0.0, 1.0, a)
    rows_a[0] = b * over_e
    rows_a[1] = a * over_e
    rows_a[2] = b * over_a
    rows_a[3] = e * over_a
    one = jnp.ones((1, 128), F32)
    nil = jnp.zeros((1, 128), F32)
    prior, now = nil, one
    rows_a[4, 0:1, :] = now
    for j in range(ROWS - 1):
        prior, now = now, rows_a[0, j : j + 1, :] * now + rows_a[1, j : j + 1, :] * prior
        rows_a[4, j + 1 : j + 2, :] = now
    prior, now = nil, one
    rows_a[5, ROWS - 1 : ROWS, :] = nil
    rows_a[5, ROWS - 2 : ROWS - 1, :] = now
    for j in range(ROWS - 2, -1, -1):
        prior, now = now, rows_a[2, j : j + 1, :] * now + rows_a[3, j : j + 1, :] * prior
        if j > 0:
            rows_a[5, j - 1 : j, :] = now
    phi = rows_a[4]
    psi = rows_a[5]
    lower_spike = jnp.where(block_lane == 0, 0.0, psi / now)
    upper_spike = phi / phi[ROWS - 1 : ROWS]
    wronskian = e * (phi * pltpu.roll(psi, ROWS - 1, 0) - pltpu.roll(phi, ROWS - 1, 0) * psi)
    wronskian = jnp.where(iota((ROWS, 128), 0) == ROWS - 1, 1.0, wronskian)

    def own(x):
        picked = jnp.where(block_lane == me, x, 0.0)
        return jnp.broadcast_to(jnp.sum(picked, axis=1, keepdims=True), (ROWS, 128))

    row = iota((ROWS, 128), 0)

    def as_row(x):
        return jnp.sum(jnp.where(row == lane, x, 0.0), axis=0, keepdims=True)

    phi_o, psi_o, wr_o = own(phi), own(psi), own(wronskian)
    a_o, b_o, e_o, l_o, u_o = own(a), own(b), own(e), own(l), own(u)
    sl_o, sr_o, weight_o = own(lower_spike), own(upper_spike), own(weight)
    phi_w = as_row(phi_o / wr_o)
    psi_w = as_row(psi_o / wr_o)
    green = jnp.where(row <= lane, phi_o * psi_w, psi_o * phi_w)
    green = jnp.where((row < ROWS - 1) & (lane < ROWS - 1), green, 0.0)
    a_end, b_end, e_end = a_o[31:32], b_o[31:32], e_o[31:32]
    ratio = jnp.where(e_end == 0.0, 0.0, u_o[31:32] / jnp.where(e_end == 0.0, 1.0, e_end))
    bend = ratio * a_end - l_o[31:32]
    tip = (lane[0:1] == ROWS - 1).astype(F32)
    local = green - l_o * pltpu.roll(green, 1, 0) - u_o * pltpu.roll(green, ROWS - 1, 0)
    end_row = bend * green[30:31] - ratio * tip
    local = jnp.where(row == ROWS - 1, end_row, local)
    pair_row = iota((8, 128), 0)
    pair = jnp.where(
        pair_row == 0,
        tip - a_end * green[30:31],
        jnp.where(pair_row == 1, green[0:1], 0.0),
    )
    shaped = jnp.concatenate([local, pair], axis=0) * as_row(weight_o)
    op = 6.0 * shaped
    op = op - 4.0 * (pltpu.roll(shaped, 1, 1) + pltpu.roll(shaped, 127, 1))
    op = op + (pltpu.roll(shaped, 2, 1) + pltpu.roll(shaped, 126, 1))
    wide = iota((40, 128), 1)
    op = jnp.where(
        wide < 34, op, jnp.where((wide >= 38) & (wide < 40), pltpu.roll(op, 40, 1), 0.0)
    )
    op_high = op.astype(BF16).astype(F32)
    op_low = op - op_high
    packed = jnp.where(wide < 32, op_high, 0.0)
    packed = jnp.where((wide >= 32) & (wide < 64), pltpu.roll(op_high, 32, 1), packed)
    packed = jnp.where((wide >= 64) & (wide < 96), pltpu.roll(op_low, 64, 1), packed)
    packed = jnp.where((wide >= 96) & (wide < 104), pltpu.roll(op_high, 64, 1), packed)
    packed = jnp.where((wide >= 104) & (wide < 112), pltpu.roll(op_high, 72, 1), packed)
    packed = jnp.where((wide >= 112) & (wide < 120), pltpu.roll(op_low, 80, 1), packed)
    wmat[0:40] = packed.astype(BF16)

    sl_before = jnp.where(row == 0, jnp.where(me == 0, 0.0, 1.0), pltpu.roll(sl_o, 1, 0))
    sl_after = jnp.where(row >= ROWS - 2, 0.0, pltpu.roll(sl_o, ROWS - 1, 0))
    sr_before = jnp.where(row == 0, 0.0, pltpu.roll(sr_o, 1, 0))
    sr_after = pltpu.roll(sr_o, ROWS - 1, 0)
    tab[0] = jnp.where(row == ROWS - 1, bend * sl_o[30:31], sl_o - l_o * sl_before - u_o * sl_after)
    tab[1] = jnp.where(
        row == ROWS - 1,
        1.0 + ratio * b_end + bend * sr_o[30:31],
        sr_o - l_o * sr_before - u_o * sr_after,
    )

    @pl.when(me == 0)
    def _():
        ytop[...] = jnp.zeros(ytop.shape, F32)

    @pl.when(me == blocks - 1)
    def _():
        ybot[...] = jnp.zeros(ybot.shape, F32)

    def pair_out(z, h):
        return pltpu.make_async_remote_copy(
            pqs.at[z, h],
            rbuf.at[me],
            p_send.at[2 * z + h],
            p_recv.at[me],
            device_id=(gx, 2 * z + h),
            device_id_type=MESH,
        )

    def pair_own(z, h):
        return pltpu.make_async_copy(pqs.at[z, h], rbuf.at[me], p_recv.at[me])

    def pair_arrival(k):
        return pltpu.make_async_remote_copy(
            pqs.at[0, 0],
            rbuf.at[k],
            p_send.at[0],
            p_recv.at[k],
            device_id=(gx, me),
            device_id_type=MESH,
        )

    @pl.loop(0, planes)
    def _(step):
        z = plane_of(step)

        @pl.when(me > 0)
        def _():
            top_out(z).wait_recv()

        @pl.when(me < blocks - 1)
        def _():
            bottom_out(z).wait_recv()

        weights = wmat[...]
        gap = jnp.zeros((4, COLS), F32)
        for f in range(FIELDS):
            source = sx[z, f]
            high, low = split(source)
            halo = jnp.concatenate([ybot[z, f], gap, ytop[z, f]], axis=0)
            halo_high = halo.astype(BF16).astype(F32)
            halo_low = halo - halo_high
            halos = jnp.concatenate([halo_high, halo_low], axis=0).astype(BF16)
            again = jnp.concatenate([halo_high, jnp.zeros((8, COLS), F32)], axis=0).astype(BF16)
            stack = jnp.concatenate([high, low, high, halos, again], axis=0)
            out = jnp.dot(weights, stack, preferred_element_type=F32)
            zl[z, f] = source - out[0:ROWS]
            for h in range(2):
                cols = slice(128 * h, 128 * h + 128)
                pqs[z, h, 0, f : f + 1, :] = out[ROWS : ROWS + 1, cols]
                pqs[z, h, 1, f : f + 1, :] = out[ROWS + 1 : ROWS + 2, cols]
        for h in range(2):

            @pl.when(2 * z + h == me)
            def _():
                pair_own(z, h).start()

            @pl.when(2 * z + h != me)
            def _():
                pair_out(z, h).start()

    col = iota((ROWS, 128), 0)

    def as_column(x):
        picked = jnp.where(col == lane, x, 0.0)
        return jnp.broadcast_to(jnp.sum(picked, axis=1, keepdims=True), (ROWS, 128))

    next_low = pltpu.roll(lower_spike[0:1], 127, 1)
    next_high = pltpu.roll(upper_spike[0:1], 127, 1)
    lanes_one = lane[0:1]
    inside = lanes_one < blocks - 1
    e_cut = jnp.where(inside, e[31:32], 0.0)
    low_band = jnp.where(lanes_one < blocks, a[31:32] * lower_spike[30:31], 0.0)
    mid_band = (
        b[31:32] + a[31:32] * upper_spike[30:31] + jnp.where(inside, e[31:32] * next_low, 0.0)
    )
    mid_band = jnp.where(lanes_one < blocks, mid_band, 1.0)
    up_band = jnp.where(inside, e[31:32] * next_high, 0.0)
    low_c, mid_c, up_c = as_column(low_band), as_column(mid_band), as_column(up_band)
    tab[2] = as_column(e_cut)
    over_up = -1.0 / jnp.where(up_c == 0.0, 1.0, up_c)
    over_low = -1.0 / jnp.where(low_c == 0.0, 1.0, low_c)
    rows_b[0] = low_c
    rows_b[1] = mid_c
    rows_b[2] = over_up
    rows_b[3] = mid_c * over_low
    rows_b[4] = up_c * over_low
    prior, now = nil, one
    for k in range(blocks):
        turn = rows_b[0, k : k + 1, :] * prior + rows_b[1, k : k + 1, :] * now
        rows_b[5, k : k + 1, :] = now
        rows_b[6, k : k + 1, :] = turn
        prior, now = now, turn * rows_b[2, k : k + 1, :]
    prior, now = nil, one
    for k in range(blocks - 1, -1, -1):
        rows_b[7, k : k + 1, :] = now
        rows_b[8, k : k + 1, :] = prior
        prior, now = now, rows_b[3, k : k + 1, :] * now + rows_b[4, k : k + 1, :] * prior
    phi_b, psi_b = rows_b[5], rows_b[7]
    scale = 1.0 / (psi_b * rows_b[6] + up_c * phi_b * rows_b[8])
    tab[3] = phi_b * scale
    tab[4] = psi_b * scale
    tab[5] = phi_b
    tab[6] = psi_b

    @pl.loop(0, blocks)
    def _(step):
        pair_arrival(lax.rem(me + step, blocks)).wait_recv()

    right_sides = []
    for k in range(blocks):
        side_k = rbuf[k, 0]
        if k < blocks - 1:
            side_k = side_k - tab[2, k : k + 1, :] * rbuf[k + 1, 1]
        right_sides.append(side_k)
    tail = jnp.zeros((FIELDS, 128), F32)
    for k in range(blocks - 1, -1, -1):
        ss[k + 1] = tab[5, k : k + 1, :] * tail
        tail = tail + tab[4, k : k + 1, :] * right_sides[k]
    head = jnp.zeros((FIELDS, 128), F32)
    ss[0] = head
    for k in range(blocks):
        head = head + tab[3, k : k + 1, :] * right_sides[k]
        ss[k + 1] = ss[k + 1] + tab[6, k : k + 1, :] * head

    def sep_out(k):
        return pltpu.make_async_remote_copy(
            ss.at[pl.ds(k, 2)],
            sbuf.at[me],
            s_send.at[k],
            s_recv.at[me],
            device_id=(gx, k),
            device_id_type=MESH,
        )

    def sep_arrival(k):
        return pltpu.make_async_remote_copy(
            ss.at[pl.ds(0, 2)],
            sbuf.at[k],
            s_send.at[0],
            s_recv.at[k],
            device_id=(gx, me),
            device_id_type=MESH,
        )

    own_copy = pltpu.make_async_copy(ss.at[pl.ds(me, 2)], sbuf.at[me], s_recv.at[me])

    @pl.loop(1, blocks)
    def _(step):
        sep_out(lax.rem(me + step, blocks)).start()

    own_copy.start()

    @pl.loop(0, planes)
    def _(step):
        z = plane_of(step)
        for h in range(2):
            k = 2 * z + h
            cols = slice(128 * h, 128 * h + 128)
            sep_arrival(k).wait_recv()
            for f in range(FIELDS):
                under = sbuf[k, 0, f : f + 1, :]
                over = sbuf[k, 1, f : f + 1, :]
                zl[z, f, :, cols] = zl[z, f, :, cols] - tab[0] * under - tab[1] * over
        pltpu.make_async_copy(zl.at[z], new_state.at[:, z], ns_sem.at[z]).start()

    @pl.loop(0, planes)
    def _(z):
        pltpu.make_async_copy(zl.at[z], new_state.at[:, z], ns_sem.at[z]).wait()
        pltpu.make_async_copy(inc.at[z], new_inc.at[:, z], ni_sem.at[z]).wait()

        @pl.when(me < blocks - 1)
        def _():
            top_out(z).wait_send()

        @pl.when(me > 0)
        def _():
            bottom_out(z).wait_send()

        for h in range(2):

            @pl.when(2 * z + h != me)
            def _():
                pair_out(z, h).wait_send()

    @pl.loop(1, blocks)
    def _(step):
        coef_out(step).wait_send()
        sep_out(lax.rem(me + step, blocks)).wait_send()


def shards(state, increment, jacobian, filter_alpha, filter_beta):
    fields, planes, rows, cols = state.shape
    blocks = lax.axis_size("gy")
    widths = lax.axis_size("gx")
    groups = planes // 4
    coef = jnp.concatenate(
        [filter_alpha, filter_beta, jnp.zeros((128 - 2 * rows,), F32)]
    ).reshape(1, 128)
    jac = jacobian.reshape(fields * fields, rows)
    full = (planes, fields, rows, cols)
    dma = pltpu.SemaphoreType.DMA
    out = jax.ShapeDtypeStruct(state.shape, F32)
    return pl.pallas_call(
        functools.partial(kernel, blocks, planes, widths),
        out_shape=(out, out),
        in_specs=[
            pl.BlockSpec(memory_space=pl.ANY),
            pl.BlockSpec(memory_space=pl.ANY),
            pl.BlockSpec(memory_space=pltpu.VMEM),
            pl.BlockSpec(memory_space=pltpu.VMEM),
        ],
        out_specs=(pl.BlockSpec(memory_space=pl.ANY), pl.BlockSpec(memory_space=pl.ANY)),
        scratch_shapes=[
            pltpu.VMEM(full, F32),
            pltpu.VMEM(full, F32),
            pltpu.VMEM(full, F32),
            pltpu.VMEM(full, F32),
            pltpu.VMEM(full, F32),
            pltpu.VMEM((fields * fields, rows, 128), F32),
            pltpu.VMEM((cols, cols), BF16),
            pltpu.VMEM((128, cols), BF16),
            pltpu.VMEM((groups, rows, 128), F32),
            pltpu.VMEM((groups, rows, 128), F32),
            pltpu.VMEM((groups, rows, 128), F32),
            pltpu.VMEM((groups, rows, 128), F32),
            pltpu.VMEM((planes, fields, 2, cols), F32),
            pltpu.VMEM((planes, fields, 2, cols), F32),
            pltpu.VMEM((planes, fields, 2, cols), F32),
            pltpu.VMEM((planes, fields, 2, cols), F32),
            pltpu.VMEM((blocks, 1, 128), F32),
            pltpu.VMEM((128, 128), F32),
            pltpu.VMEM((7, rows, 128), F32),
            pltpu.VMEM((6, rows, 128), F32),
            pltpu.VMEM((9, rows, 128), F32),
            pltpu.VMEM((planes, 2, 2, fields, 128), F32),
            pltpu.VMEM((blocks, 2, fields, 128), F32),
            pltpu.VMEM((blocks + 1, fields, 128), F32),
            pltpu.VMEM((blocks, 2, fields, 128), F32),
            pltpu.VMEM((40, 128), BF16),
            dma((planes,)),
            dma((planes,)),
            dma((planes,)),
            dma((planes,)),
            dma((1,)),
            dma((2,)),
            dma((2,)),
            dma((blocks,)),
            dma((blocks,)),
            dma((planes,)),
            dma((planes,)),
            dma((planes,)),
            dma((planes,)),
            dma((blocks,)),
            dma((blocks,)),
            dma((blocks,)),
            dma((blocks,)),
        ],
        compiler_params=pltpu.CompilerParams(
            collective_id=0, has_side_effects=True, vmem_limit_bytes=60 * 1024 * 1024
        ),
    )(state, increment, coef, jac)


def solution(mesh):
    placed = (
        P(None, None, "gy", "gx"),
        P(None, None, "gy", "gx"),
        P(None, None, "gy"),
        P("gy"),
        P("gy"),
    )
    return jax.shard_map(
        shards,
        mesh=mesh,
        in_specs=placed,
        out_specs=(P(None, None, "gy", "gx"), P(None, None, "gy", "gx")),
        check_vma=False,
    )
```

```python
import functools

import jax
import jax.numpy as jnp
from jax import lax
from jax.experimental import pallas as pl
from jax.experimental.pallas import tpu as pltpu
from jax.sharding import PartitionSpec as P

section_a = -5.0 / 9.0
section_b = 15.0 / 16.0
courant = 0.5
MESH = pl.DeviceIdType.MESH
F32 = jnp.float32
BF16 = jnp.bfloat16
FIELDS = 5
ROWS = 32
MESSAGE = 11
COLS = 256


def iota(shape, dim):
    return lax.broadcasted_iota(jnp.int32, shape, dim)


def split(x):
    high = x.astype(BF16)
    return high, (x - high.astype(F32)).astype(BF16)


def stencil_weights():
    gap = iota((COLS, COLS), 0) - iota((COLS, COLS), 1)
    size = jnp.abs(gap)
    weight = jnp.where(size == 1, 45.0, jnp.where(size == 2, -9.0, jnp.where(size == 3, 1.0, 0.0)))
    return jnp.where(gap < 0, -weight, weight)


def before(x):
    rolled = pltpu.roll(x, 1, 0)
    return jnp.where(iota(x.shape, 0) == 0, pltpu.roll(rolled, 1, 1), rolled)


def after(x):
    rolled = pltpu.roll(x, ROWS - 1, 0)
    return jnp.where(iota(x.shape, 0) == ROWS - 1, pltpu.roll(rolled, 127, 1), rolled)


def factors(alpha, beta, point, last):
    inner = (point >= 1) & (point < last)
    low_one = jnp.where((point >= 1) & (point <= last), alpha, 0.0)
    up_one = jnp.where(point < last, alpha, 0.0)
    low_two = jnp.where(inner, after(beta), 0.0)
    up_two = jnp.where(inner, before(beta), 0.0)
    a, e, b = low_one, up_one, jnp.ones(alpha.shape, F32)
    for _ in range(3):
        l = low_two / jnp.where(inner, after(a), 1.0)
        u = up_two / jnp.where(inner, before(e), 1.0)
        a = low_one - b * l
        e = up_one - b * u
        b = (
            1.0
            - a * jnp.where(point >= 1, before(u), 0.0)
            - e * jnp.where(point < last, after(l), 0.0)
        )
    return a, b, e, l, u


def kernel(
    blocks,
    planes,
    widths,
    state,
    increment,
    alpha_ref,
    beta_ref,
    jac_ref,
    zl,
    nin,
    sbuf,
    spikes,
    st,
    inc,
    gr,
    sx,
    jb,
    jv,
    dxw,
    xs,
    hl,
    hr,
    ytop_s,
    ybot_s,
    ytop,
    ybot,
    av,
    cs,
    cb,
    sq,
    rows_a,
    rows_b,
    pqs,
    rbuf,
    ss,
    wmat,
    st_sem,
    inc_sem,
    in_sem,
    z_sem,
    y_sem,
    x_send,
    x_recv,
    c_send,
    c_recv,
    yt_send,
    yt_recv,
    yb_send,
    yb_recv,
    p_send,
    p_recv,
    s_send,
    s_recv,
):
    gx = lax.axis_index("gx")
    me = lax.axis_index("gy")
    left = lax.rem(gx + widths - 1, widths)
    right = lax.rem(gx + 1, widths)
    groups = planes // 4
    home = me // 2
    ring = max(blocks // 4, 1)
    sheets = blocks // ring
    rounds = max(ring // 2 - 1, 0)
    gz = lax.rem(me, ring)
    gq = me // ring
    z_near = [gq * ring + lax.rem(gz + move, ring) for move in (1, ring - 1)]
    y_near = [lax.rem(gq + move, sheets) * ring + gz for move in (1, sheets - 1)]
    after_me = lax.rem(me + 1, blocks)
    before_me = lax.rem(me + blocks - 1, blocks)
    lane = iota((ROWS, 128), 1)
    row = iota((ROWS, 128), 0)

    barrier = pltpu.get_barrier_semaphore()
    for peer in [(left, me), (right, me)] + [
        (gx, other) for other in z_near + y_near + [after_me, before_me]
    ]:
        pl.semaphore_signal(barrier, inc=1, device_id=peer, device_id_type=MESH)

    def tell(sem, peers):
        for other in peers:
            pl.semaphore_signal(sem, inc=1, device_id=(gx, other), device_id_type=MESH)

    def plane_of(step):
        return lax.rem(step + home + 2, planes)

    def state_in(z):
        return pltpu.make_async_copy(state.at[:, z], st.at[z], st_sem.at[z])

    def inc_in(z):
        return pltpu.make_async_copy(increment.at[:, z], inc.at[z], inc_sem.at[z])

    @pl.loop(0, planes)
    def _(z):
        state_in(z).start()

    small_in = [
        pltpu.make_async_copy(alpha_ref, av.at[0], in_sem.at[0]),
        pltpu.make_async_copy(beta_ref, av.at[1], in_sem.at[1]),
        pltpu.make_async_copy(jac_ref, jv, in_sem.at[2]),
    ]
    for copy in small_in:
        copy.start()

    @pl.loop(0, planes)
    def _(step):
        inc_in(plane_of(step)).start()

    @pl.loop(0, groups)
    def _(g):
        edges = jnp.zeros((ROWS, 128), F32)
        for q in range(4):
            z = g * 4 + q
            state_in(z).wait()
            for f in range(FIELDS):
                base = q * 32 + f * 6
                ends = jnp.where(lane < 64, st[z, f, :, 0:128], st[z, f, :, 128:256])
                moved = pltpu.roll(ends, base + 3, 1)
                edges = jnp.where((lane >= base) & (lane < base + 6), moved, edges)
        xs[g] = edges

    for copy in small_in:
        copy.wait()
    cs[...] = jnp.zeros((1, 128), F32)
    cs[:, 0:ROWS] = av[0]
    cs[:, ROWS : 2 * ROWS] = av[1]

    pl.semaphore_wait(barrier, 8)

    send_left = pltpu.make_async_remote_copy(
        xs, hr, x_send.at[0], x_recv.at[0], device_id=(left, me), device_id_type=MESH
    )
    send_right = pltpu.make_async_remote_copy(
        xs, hl, x_send.at[1], x_recv.at[1], device_id=(right, me), device_id_type=MESH
    )
    send_left.start()
    send_right.start()
    if rounds > 0:
        tell(z_sem.at[0], z_near)
    near_coefs = [
        pltpu.make_async_remote_copy(
            cs,
            cb.at[i],
            c_send.at[i],
            c_recv.at[i],
            device_id=(gx, other),
            device_id_type=MESH,
        )
        for i, other in enumerate([after_me, before_me])
    ]
    for copy in near_coefs:
        copy.start()

    dxw[...] = stencil_weights().astype(BF16)
    sq[...] = jnp.zeros((128, 128), F32)
    for f in range(FIELDS):
        sq[8 * f : 8 * f + FIELDS, 0:ROWS] = jv[f]
    jac_t = sq[...].T
    for f in range(FIELDS):
        for g in range(FIELDS):
            pick = jac_t[0:ROWS, 8 * f + g : 8 * f + g + 1]
            jb[f * FIELDS + g] = jnp.broadcast_to(pick, (ROWS, 128)) * (courant / 60.0)

    def gradient(z):
        high, low = split(st[z].reshape(FIELDS * ROWS, COLS))
        weights = dxw[...]
        total = jnp.dot(high, weights, preferred_element_type=F32) + jnp.dot(
            low, weights, preferred_element_type=F32
        )
        gr[z] = total.reshape(FIELDS, ROWS, COLS)

    pl.loop(0, planes // 2)(gradient)
    if rounds > 0:
        pl.semaphore_wait(z_sem.at[0], 2)
    if rounds > 1:
        tell(z_sem.at[1], z_near)
    pl.loop(planes // 2, planes)(gradient)
    if rounds > 1:
        pl.semaphore_wait(z_sem.at[1], 2)
    if rounds > 2:
        tell(z_sem.at[2], z_near)
    for copy in near_coefs:
        copy.wait()

    sq[...] = jnp.zeros((128, 128), F32)
    sq[0:1, :] = cb[0]
    sq[1:2, :] = cs[...]
    sq[2:3, :] = cb[1]
    turned = sq[...].T
    alpha = turned[0:ROWS]
    beta = turned[ROWS : 2 * ROWS]
    last = ROWS * blocks - 1
    a, b, e, l, u = factors(alpha, beta, row + ROWS * (lane + me - 1), last)
    weight = (1.0 - 2.0 * alpha + 2.0 * beta) * (1.0 / 16.0)

    def own(x):
        return jnp.broadcast_to(x[:, 1:2], x.shape)

    a_o, b_o, e_o, l_o, u_o, weight_o = [own(x) for x in (a, b, e, l, u, weight)]
    over_e = -1.0 / jnp.where(e_o == 0.0, 1.0, e_o)
    over_a = -1.0 / jnp.where(a_o == 0.0, 1.0, a_o)
    rows_a[0] = b_o * over_e
    rows_a[1] = a_o * over_e
    rows_a[2] = b_o * over_a
    rows_a[3] = e_o * over_a
    one = jnp.ones((1, 128), F32)
    nil = jnp.zeros((1, 128), F32)
    prior, now = nil, one
    prior_d, now_d = nil, one
    rows_a[4, 0:1, :] = now
    rows_a[5, ROWS - 1 : ROWS, :] = nil
    rows_a[5, ROWS - 2 : ROWS - 1, :] = now_d
    for j in range(ROWS - 1):
        prior, now = now, rows_a[0, j : j + 1, :] * now + rows_a[1, j : j + 1, :] * prior
        rows_a[4, j + 1 : j + 2, :] = now
        i = ROWS - 2 - j
        prior_d, now_d = (
            now_d,
            rows_a[2, i : i + 1, :] * now_d + rows_a[3, i : i + 1, :] * prior_d,
        )
        if i > 0:
            rows_a[5, i - 1 : i, :] = now_d
    phi_o = rows_a[4]
    psi_o = rows_a[5]
    sl_o = jnp.where(me == 0, 0.0, psi_o / now_d)
    sr_o = phi_o / now
    wr_o = e_o * (
        phi_o * pltpu.roll(psi_o, ROWS - 1, 0) - pltpu.roll(phi_o, ROWS - 1, 0) * psi_o
    )
    wr_o = 1.0 / jnp.where(row == ROWS - 1, 1.0, wr_o)

    def as_row(x):
        return jnp.sum(jnp.where(row == lane, x, 0.0), axis=0, keepdims=True)

    phi_w = as_row(phi_o * wr_o)
    psi_w = as_row(psi_o * wr_o)
    green = jnp.where(row <= lane, phi_o * psi_w, psi_o * phi_w)
    green = jnp.where((row < ROWS - 1) & (lane < ROWS - 1), green, 0.0)
    a_end, b_end, e_end = a_o[31:32], b_o[31:32], e_o[31:32]
    ratio = jnp.where(e_end == 0.0, 0.0, u_o[31:32] / jnp.where(e_end == 0.0, 1.0, e_end))
    bend = ratio * a_end - l_o[31:32]
    tip = (lane[0:1] == ROWS - 1).astype(F32)
    local = green - l_o * pltpu.roll(green, 1, 0) - u_o * pltpu.roll(green, ROWS - 1, 0)
    end_row = bend * green[30:31] - ratio * tip
    local = jnp.where(row == ROWS - 1, end_row, local)
    pair_row = iota((8, 128), 0)
    pair = jnp.where(
        pair_row == 0,
        tip - a_end * green[30:31],
        jnp.where(pair_row == 1, green[0:1], 0.0),
    )
    shaped = jnp.concatenate([local, pair], axis=0) * as_row(weight_o)
    op = 6.0 * shaped
    op = op - 4.0 * (pltpu.roll(shaped, 1, 1) + pltpu.roll(shaped, 127, 1))
    op = op + (pltpu.roll(shaped, 2, 1) + pltpu.roll(shaped, 126, 1))
    wide = iota((40, 128), 1)
    op = jnp.where(
        wide < 34, op, jnp.where((wide >= 38) & (wide < 40), pltpu.roll(op, 40, 1), 0.0)
    )
    op_high = op.astype(BF16).astype(F32)
    op_low = op - op_high
    packed = jnp.where(wide < 32, op_high, 0.0)
    packed = jnp.where((wide >= 32) & (wide < 64), pltpu.roll(op_high, 32, 1), packed)
    packed = jnp.where((wide >= 64) & (wide < 96), pltpu.roll(op_low, 64, 1), packed)
    packed = jnp.where((wide >= 96) & (wide < 104), pltpu.roll(op_high, 64, 1), packed)
    packed = jnp.where((wide >= 104) & (wide < 112), pltpu.roll(op_high, 72, 1), packed)
    packed = jnp.where((wide >= 112) & (wide < 120), pltpu.roll(op_low, 80, 1), packed)
    wmat[...] = packed.astype(BF16)

    sl_before = jnp.where(row == 0, jnp.where(me == 0, 0.0, 1.0), pltpu.roll(sl_o, 1, 0))
    sl_after = jnp.where(row >= ROWS - 2, 0.0, pltpu.roll(sl_o, ROWS - 1, 0))
    sr_before = jnp.where(row == 0, 0.0, pltpu.roll(sr_o, 1, 0))
    sr_after = pltpu.roll(sr_o, ROWS - 1, 0)
    spikes[0] = jnp.where(
        row == ROWS - 1, bend * sl_o[30:31], sl_o - l_o * sl_before - u_o * sl_after
    )
    spikes[1] = jnp.where(
        row == ROWS - 1,
        1.0 + ratio * b_end + bend * sr_o[30:31],
        sr_o - l_o * sr_before - u_o * sr_after,
    )

    tags = [a_end * sl_o[30:31], b_end + a_end * sr_o[30:31], e_end, sl_o[0:1], sr_o[0:1]]
    tag = nil
    for i, value in enumerate(tags):
        tag = jnp.where(lane[0:1] == i, value, tag)

    @pl.loop(0, planes)
    def _(z):
        for h in range(2):
            pqs[z, h, MESSAGE - 1 : MESSAGE, :] = tag

    @pl.when(me == 0)
    def _():
        ytop[...] = jnp.zeros(ytop.shape, F32)

    @pl.when(me == blocks - 1)
    def _():
        ybot[...] = jnp.zeros(ybot.shape, F32)

    if rounds > 2:
        pl.semaphore_wait(z_sem.at[2], 2)
    tell(y_sem.at[0], y_near)
    send_left.wait()
    send_right.wait()

    spot = lax.rem(lax.rem(lane, 32), 6)
    for g in range(groups):
        halo = jnp.where(spot < 3, hl[g], hr[g])
        total = jnp.zeros((ROWS, 128), F32)
        for gap, factor in ((1, 45.0), (2, -9.0), (3, 1.0)):
            from_left = (spot >= 3) & (spot < 3 + gap)
            from_right = (spot >= 3 - gap) & (spot < 3)
            total = total - jnp.where(from_left, factor * pltpu.roll(halo, gap, 1), 0.0)
            total = total + jnp.where(from_right, factor * pltpu.roll(halo, 128 - gap, 1), 0.0)
        xs[g] = total

    def top_out(z):
        return pltpu.make_async_remote_copy(
            ytop_s.at[z],
            ytop.at[z],
            yt_send.at[z],
            yt_recv.at[z],
            device_id=(gx, after_me),
            device_id_type=MESH,
        )

    def bottom_out(z):
        return pltpu.make_async_remote_copy(
            ybot_s.at[z],
            ybot.at[z],
            yb_send.at[z],
            yb_recv.at[z],
            device_id=(gx, before_me),
            device_id_type=MESH,
        )

    def section(step):
        z = plane_of(step)
        inc_in(z).wait()
        edges = xs[z // 4]
        offset = lax.rem(z, 4) * 32
        edge = [
            pltpu.roll(edges, lax.rem(253 - 6 * f - offset, 128), 1) for f in range(FIELDS)
        ]
        for h in range(2):
            cols = slice(128 * h, 128 * h + 128)
            near = lane < 3 if h == 0 else lane >= 125
            grads = [
                gr[z, f, :, cols] + jnp.where(near, edge[f], 0.0) for f in range(FIELDS)
            ]
            for f in range(FIELDS):
                flux = jb[f * FIELDS] * grads[0]
                for other in range(1, FIELDS):
                    flux = flux + jb[f * FIELDS + other] * grads[other]
                fresh = section_a * inc[z, f, :, cols] - flux
                source = st[z, f, :, cols] + section_b * fresh
                nin[z, f, :, cols] = fresh
                sx[z, f, :, cols] = source
                ybot_s[z, f, :, cols] = source[0:2]
                ytop_s[z, f, :, cols] = source[ROWS - 2 : ROWS]

        @pl.when(me < blocks - 1)
        def _():
            top_out(z).start()

        @pl.when(me > 0)
        def _():
            bottom_out(z).start()

    pl.loop(0, planes // 2)(section)
    pl.semaphore_wait(y_sem.at[0], 2)
    tell(y_sem.at[1], y_near)
    pl.loop(planes // 2, planes)(section)
    pl.semaphore_wait(y_sem.at[1], 2)

    def pair_out(z, h):
        return pltpu.make_async_remote_copy(
            pqs.at[z, h],
            rbuf.at[me],
            p_send,
            p_recv,
            device_id=(gx, 2 * z + h),
            device_id_type=MESH,
        )

    def pair_own(z, h):
        return pltpu.make_async_copy(pqs.at[z, h], rbuf.at[me], p_recv)

    @pl.loop(0, planes)
    def _(step):
        z = plane_of(step)

        @pl.when(me > 0)
        def _():
            top_out(z).wait_recv()

        @pl.when(me < blocks - 1)
        def _():
            bottom_out(z).wait_recv()

        weights = wmat[...]
        gap = jnp.zeros((4, COLS), F32)
        for f in range(FIELDS):
            source = sx[z, f]
            high, low = split(source)
            halo = jnp.concatenate([ybot[z, f], gap, ytop[z, f]], axis=0)
            halo_high = halo.astype(BF16).astype(F32)
            halo_low = halo - halo_high
            halos = jnp.concatenate([halo_high, halo_low], axis=0).astype(BF16)
            again = jnp.concatenate([halo_high, jnp.zeros((8, COLS), F32)], axis=0).astype(BF16)
            stack = jnp.concatenate([high, low, high, halos, again], axis=0)
            out = jnp.dot(weights, stack, preferred_element_type=F32)
            zl[z, f] = source - out[0:ROWS]
            for h in range(2):
                cols = slice(128 * h, 128 * h + 128)
                pqs[z, h, f : f + 1, :] = out[ROWS : ROWS + 1, cols]
                pqs[z, h, FIELDS + f : FIELDS + f + 1, :] = out[ROWS + 1 : ROWS + 2, cols]
        for h in range(2):

            @pl.when(2 * z + h == me)
            def _():
                pair_own(z, h).start()

            @pl.when(2 * z + h != me)
            def _():
                pair_out(z, h).start()

    @pl.loop(0, planes)
    def _(z):
        @pl.when(me < blocks - 1)
        def _():
            top_out(z).wait_send()

        @pl.when(me > 0)
        def _():
            bottom_out(z).wait_send()

    pltpu.make_async_copy(rbuf, rbuf, p_recv).wait()

    tagged = jnp.concatenate([rbuf[k, MESSAGE - 1 : MESSAGE, :] for k in range(blocks)], axis=0)
    block = iota((blocks, 128), 0)

    def quantity(i):
        return jnp.broadcast_to(tagged[:, i : i + 1], (blocks, 128))

    def following(x):
        return jnp.where(block == blocks - 1, 0.0, pltpu.roll(x, blocks - 1, 0))

    e_cut = quantity(2)
    low_c = quantity(0)
    mid_c = quantity(1) + e_cut * following(quantity(3))
    up_c = e_cut * following(quantity(4))
    over_up = -1.0 / jnp.where(up_c == 0.0, 1.0, up_c)
    over_low = -1.0 / jnp.where(low_c == 0.0, 1.0, low_c)
    rows_b[0] = low_c * over_up
    rows_b[1] = mid_c * over_up
    rows_b[2] = mid_c * over_low
    rows_b[3] = up_c * over_low
    rows_b[4, 0:1, :] = one
    rows_b[5, blocks - 1 : blocks, :] = one
    prior, now = nil, one
    prior_d, now_d = nil, one
    for k in range(blocks - 1):
        prior, now = now, rows_b[0, k : k + 1, :] * prior + rows_b[1, k : k + 1, :] * now
        rows_b[4, k + 1 : k + 2, :] = now
        i = blocks - 1 - k
        prior_d, now_d = (
            now_d,
            rows_b[2, i : i + 1, :] * now_d + rows_b[3, i : i + 1, :] * prior_d,
        )
        rows_b[5, i - 1 : i, :] = now_d
    phi_b, psi_b = rows_b[4], rows_b[5]
    leading = jnp.where(block == 0, 0.0, pltpu.roll(phi_b, 1, 0))
    turn = low_c * leading + mid_c * phi_b
    scale = 1.0 / (psi_b * turn + up_c * phi_b * following(psi_b))
    rows_b[6] = phi_b * scale
    rows_b[7] = psi_b * scale
    rows_b[8] = e_cut

    right_sides = []
    for k in range(blocks):
        side_k = rbuf[k, 0:FIELDS]
        if k < blocks - 1:
            side_k = side_k - rows_b[8, k : k + 1, :] * rbuf[k + 1, FIELDS : 2 * FIELDS]
        right_sides.append(side_k)
    tail = jnp.zeros((FIELDS, 128), F32)
    for k in range(blocks - 1, -1, -1):
        ss[k + 1] = rows_b[4, k : k + 1, :] * tail
        tail = tail + rows_b[7, k : k + 1, :] * right_sides[k]
    front = jnp.zeros((FIELDS, 128), F32)
    ss[0] = front
    for k in range(blocks):
        front = front + rows_b[6, k : k + 1, :] * right_sides[k]
        ss[k + 1] = ss[k + 1] + rows_b[5, k : k + 1, :] * front

    def sep_out(step):
        k = lax.rem(me + 1 + lax.rem(step + 4, blocks - 1), blocks)
        return pltpu.make_async_remote_copy(
            ss.at[pl.ds(k, 2)],
            sbuf.at[me],
            s_send,
            s_recv,
            device_id=(gx, k),
            device_id_type=MESH,
        )

    @pl.loop(0, blocks - 1)
    def _(step):
        sep_out(step).start()

    pltpu.make_async_copy(ss.at[pl.ds(me, 2)], sbuf.at[me], s_recv).start()

    sent = pl.ds(0, blocks - 1)
    pltpu.make_async_copy(rbuf.at[sent], rbuf.at[sent], p_send).wait()
    pltpu.make_async_copy(sbuf, sbuf, s_recv).wait()
    pltpu.make_async_copy(sbuf.at[sent], sbuf.at[sent], s_send).wait()


def finish(planes, zl, nin, sbuf, spikes, new_state, new_inc, ready, state_sem, inc_sem):
    def inc_out(z):
        return pltpu.make_async_copy(nin.at[z], new_inc.at[:, z], inc_sem.at[z])

    def state_out(z):
        return pltpu.make_async_copy(ready.at[z], new_state.at[:, z], state_sem.at[z])

    @pl.loop(0, planes)
    def _(z):
        inc_out(z).start()

    @pl.loop(0, planes)
    def _(z):
        for h in range(2):
            k = 2 * z + h
            cols = slice(128 * h, 128 * h + 128)
            for f in range(FIELDS):
                under = sbuf[k, 0, f : f + 1, :]
                over = sbuf[k, 1, f : f + 1, :]
                ready[z, f, :, cols] = (
                    zl[z, f, :, cols] - spikes[0] * under - spikes[1] * over
                )
        state_out(z).start()

    @pl.loop(0, planes)
    def _(z):
        state_out(z).wait()
        inc_out(z).wait()


def shards(state, increment, jacobian, filter_alpha, filter_beta):
    fields, planes, rows, cols = state.shape
    blocks = lax.axis_size("gy")
    widths = lax.axis_size("gx")
    groups = planes // 4
    full = (planes, fields, rows, cols)
    halo = (planes, fields, 2, cols)
    dma = pltpu.SemaphoreType.DMA
    anywhere = pl.BlockSpec(memory_space=pltpu.HBM)
    near = pl.BlockSpec(memory_space=pltpu.VMEM)
    whole = jax.ShapeDtypeStruct(state.shape, F32)
    zl, nin, sbuf, spikes = pl.pallas_call(
        functools.partial(kernel, blocks, planes, widths),
        out_shape=(
            jax.ShapeDtypeStruct(full, F32),
            jax.ShapeDtypeStruct(full, F32),
            jax.ShapeDtypeStruct((blocks, 2, fields, 128), F32),
            jax.ShapeDtypeStruct((2, rows, 128), F32),
        ),
        in_specs=[anywhere] * 5,
        out_specs=(near,) * 4,
        scratch_shapes=[
            pltpu.VMEM(full, F32),
            pltpu.VMEM(full, F32),
            pltpu.VMEM(full, F32),
            pltpu.VMEM(full, F32),
            pltpu.VMEM((fields * fields, rows, 128), F32),
            pltpu.VMEM((fields, fields, rows), F32),
            pltpu.VMEM((cols, cols), BF16),
            pltpu.VMEM((groups, rows, 128), F32),
            pltpu.VMEM((groups, rows, 128), F32),
            pltpu.VMEM((groups, rows, 128), F32),
            pltpu.VMEM(halo, F32),
            pltpu.VMEM(halo, F32),
            pltpu.VMEM(halo, F32),
            pltpu.VMEM(halo, F32),
            pltpu.VMEM((2, 1, rows), F32),
            pltpu.VMEM((1, 128), F32),
            pltpu.VMEM((2, 1, 128), F32),
            pltpu.VMEM((128, 128), F32),
            pltpu.VMEM((6, rows, 128), F32),
            pltpu.VMEM((9, blocks, 128), F32),
            pltpu.VMEM((planes, 2, MESSAGE, 128), F32),
            pltpu.VMEM((blocks, MESSAGE, 128), F32),
            pltpu.VMEM((blocks + 1, fields, 128), F32),
            pltpu.VMEM((40, 128), BF16),
            dma((planes,)),
            dma((planes,)),
            dma((3,)),
            pltpu.SemaphoreType.REGULAR((3,)),
            pltpu.SemaphoreType.REGULAR((2,)),
            dma((2,)),
            dma((2,)),
            dma((2,)),
            dma((2,)),
            dma((planes,)),
            dma((planes,)),
            dma((planes,)),
            dma((planes,)),
            dma,
            dma,
            dma,
            dma,
        ],
        compiler_params=pltpu.CompilerParams(
            collective_id=0, has_side_effects=True, vmem_limit_bytes=32 * 1024 * 1024
        ),
    )(
        *[
            pltpu.with_memory_space_constraint(x, pltpu.HBM)
            for x in (
                state,
                increment,
                filter_alpha.reshape(1, rows),
                filter_beta.reshape(1, rows),
                jacobian,
            )
        ]
    )
    return pl.pallas_call(
        functools.partial(finish, planes),
        out_shape=(whole, whole),
        in_specs=[near] * 4,
        out_specs=(anywhere, anywhere),
        scratch_shapes=[pltpu.VMEM(full, F32), dma((planes,)), dma((planes,))],
        compiler_params=pltpu.CompilerParams(vmem_limit_bytes=24 * 1024 * 1024),
    )(zl, nin, sbuf, spikes)


def solution(mesh):
    placed = (
        P(None, None, "gy", "gx"),
        P(None, None, "gy", "gx"),
        P(None, None, "gy"),
        P("gy"),
        P("gy"),
    )
    return jax.shard_map(
        shards,
        mesh=mesh,
        in_specs=placed,
        out_specs=(P(None, None, "gy", "gx"), P(None, None, "gy", "gx")),
        check_vma=False,
    )
```

```python
import functools

import jax
import jax.numpy as jnp
import numpy as np
from jax import lax
from jax.experimental import pallas as pl
from jax.experimental.pallas import tpu as pltpu
from jax.sharding import PartitionSpec as P

section_a = -5.0 / 9.0
section_b = 15.0 / 16.0
courant = 0.5
MESH = pl.DeviceIdType.MESH
F32 = jnp.float32
BF16 = jnp.bfloat16
FIELDS = 5
ROWS = 32
MESSAGE = 11
COLS = 256


def iota(shape, dim):
    return lax.broadcasted_iota(jnp.int32, shape, dim)


def split(x):
    high = x.astype(BF16)
    return high, (x - high.astype(F32)).astype(BF16)


def stencil_weights():
    gap = np.arange(COLS)[:, None] - np.arange(COLS)[None, :]
    size = np.abs(gap)
    weight = np.where(size == 1, 45.0, np.where(size == 2, -9.0, np.where(size == 3, 1.0, 0.0)))
    return jnp.asarray(np.sign(gap) * weight, BF16)


def before(x):
    rolled = pltpu.roll(x, 1, 0)
    return jnp.where(iota(x.shape, 0) == 0, pltpu.roll(rolled, 1, 1), rolled)


def after(x):
    rolled = pltpu.roll(x, ROWS - 1, 0)
    return jnp.where(iota(x.shape, 0) == ROWS - 1, pltpu.roll(rolled, 127, 1), rolled)


def factors(alpha, beta, point, last):
    inner = (point >= 1) & (point < last)
    low_one = jnp.where((point >= 1) & (point <= last), alpha, 0.0)
    up_one = jnp.where(point < last, alpha, 0.0)
    low_two = jnp.where(inner, after(beta), 0.0)
    up_two = jnp.where(inner, before(beta), 0.0)
    a, e, b = low_one, up_one, jnp.ones(alpha.shape, F32)
    for _ in range(3):
        l = low_two / jnp.where(inner, after(a), 1.0)
        u = up_two / jnp.where(inner, before(e), 1.0)
        a = low_one - b * l
        e = up_one - b * u
        b = (
            1.0
            - a * jnp.where(point >= 1, before(u), 0.0)
            - e * jnp.where(point < last, after(l), 0.0)
        )
    return a, b, e, l, u


def kernel(
    blocks,
    planes,
    widths,
    state,
    increment,
    alpha_ref,
    beta_ref,
    jac_ref,
    dxw_ref,
    zl,
    nin,
    sbuf,
    spikes,
    st,
    inc,
    gr,
    sx,
    jb,
    jv,
    dxw,
    xs,
    to_left,
    to_right,
    hl,
    hr,
    ytop_s,
    ybot_s,
    ytop,
    ybot,
    av,
    cs,
    cb,
    sq,
    rows_a,
    rows_b,
    wpq,
    pqs,
    rbuf,
    ss,
    wmat,
    st_sem,
    inc_sem,
    in_sem,
    z_sem,
    y_sem,
    x_send,
    x_recv,
    c_send,
    c_recv,
    yt_send,
    yt_recv,
    yb_send,
    yb_recv,
    p_send,
    p_recv,
    s_send,
    s_recv,
):
    gx = lax.axis_index("gx")
    me = lax.axis_index("gy")
    left = lax.rem(gx + widths - 1, widths)
    right = lax.rem(gx + 1, widths)
    groups = planes // 4
    home = me // 2
    ring = max(blocks // 4, 1)
    sheets = blocks // ring
    rounds = max(ring // 2 - 1, 0)
    gz = lax.rem(me, ring)
    gq = me // ring
    z_near = [gq * ring + lax.rem(gz + move, ring) for move in (1, ring - 1)]
    y_near = [lax.rem(gq + move, sheets) * ring + gz for move in (1, sheets - 1)]
    after_me = lax.rem(me + 1, blocks)
    before_me = lax.rem(me + blocks - 1, blocks)
    lane = iota((ROWS, 128), 1)
    row = iota((ROWS, 128), 0)

    barrier = pltpu.get_barrier_semaphore()
    for peer in [(left, me), (right, me)] + [
        (gx, other) for other in z_near + y_near + [after_me, before_me]
    ]:
        pl.semaphore_signal(barrier, inc=1, device_id=peer, device_id_type=MESH)

    def tell(sem, peers):
        for other in peers:
            pl.semaphore_signal(sem, inc=1, device_id=(gx, other), device_id_type=MESH)

    def plane_of(step):
        return lax.rem(step + home + 2, planes)

    def state_in(z):
        return pltpu.make_async_copy(state.at[:, z], st.at[z], st_sem.at[z])

    def inc_in(z):
        return pltpu.make_async_copy(increment.at[:, z], inc.at[z], inc_sem.at[z])

    small_in = [
        pltpu.make_async_copy(alpha_ref, av.at[0], in_sem.at[0]),
        pltpu.make_async_copy(beta_ref, av.at[1], in_sem.at[1]),
        pltpu.make_async_copy(jac_ref, jv, in_sem.at[2]),
        pltpu.make_async_copy(dxw_ref, dxw, in_sem.at[3]),
    ]
    for copy in small_in:
        copy.start()

    @pl.loop(0, planes)
    def _(z):
        state_in(z).start()

    @pl.loop(0, planes)
    def _(step):
        inc_in(plane_of(step)).start()

    @pl.loop(0, groups)
    def _(g):
        for q in range(4):
            state_in(g * 4 + q).wait()
        edges = jnp.zeros((ROWS, 128), F32)
        for q in range(4):
            z = g * 4 + q
            for f in range(FIELDS):
                base = q * 32 + f * 6
                ends = jnp.where(lane < 64, st[z, f, :, 0:128], st[z, f, :, 128:256])
                moved = pltpu.roll(ends, base + 3, 1)
                edges = jnp.where((lane >= base) & (lane < base + 6), moved, edges)
        xs[g] = edges

    for copy in small_in:
        copy.wait()
    cs[...] = jnp.zeros((1, 128), F32)
    cs[:, 0:ROWS] = av[0]
    cs[:, ROWS : 2 * ROWS] = av[1]

    spot = lax.rem(lax.rem(lane, 32), 6)
    pairs = (groups + 1) // 2
    for p in range(pairs):
        one, two = xs[2 * p], xs[min(2 * p + 1, groups - 1)]
        to_right[p] = jnp.where(spot < 3, one, pltpu.roll(two, 3, 1))
        to_left[p] = jnp.where(spot < 3, pltpu.roll(one, 125, 1), two)

    pl.semaphore_wait(barrier, 8)

    send_left = pltpu.make_async_remote_copy(
        to_left, hr, x_send.at[0], x_recv.at[0], device_id=(left, me), device_id_type=MESH
    )
    send_right = pltpu.make_async_remote_copy(
        to_right, hl, x_send.at[1], x_recv.at[1], device_id=(right, me), device_id_type=MESH
    )
    send_left.start()
    send_right.start()
    if rounds > 0:
        tell(z_sem.at[0], z_near)
    near_coefs = [
        pltpu.make_async_remote_copy(
            cs,
            cb.at[i],
            c_send.at[i],
            c_recv.at[i],
            device_id=(gx, other),
            device_id_type=MESH,
        )
        for i, other in enumerate([after_me, before_me])
    ]
    for copy in near_coefs:
        copy.start()

    sq[...] = jnp.zeros((128, 128), F32)
    for f in range(FIELDS):
        sq[8 * f : 8 * f + FIELDS, 0:ROWS] = jv[f]
    jac_t = sq[...].T
    for f in range(FIELDS):
        for g in range(FIELDS):
            pick = jac_t[0:ROWS, 8 * f + g : 8 * f + g + 1]
            jb[f * FIELDS + g] = jnp.broadcast_to(pick, (ROWS, 128)) * (courant / 60.0)

    def gradient(step):
        z = pl.ds(4 * step, 4)
        high, low = split(st[z].reshape(4 * FIELDS * ROWS, COLS))
        weights = dxw[...]
        total = jnp.dot(high, weights, preferred_element_type=F32) + jnp.dot(
            low, weights, preferred_element_type=F32
        )
        gr[z] = total.reshape(4, FIELDS, ROWS, COLS)

    pl.loop(0, planes // 8)(gradient)
    if rounds > 0:
        pl.semaphore_wait(z_sem.at[0], 2)
    if rounds > 1:
        tell(z_sem.at[1], z_near)
    pl.loop(planes // 8, planes // 4)(gradient)
    if rounds > 1:
        pl.semaphore_wait(z_sem.at[1], 2)
    if rounds > 2:
        tell(z_sem.at[2], z_near)
    @pl.when(me == 0)
    def _():
        ytop[...] = jnp.zeros(ytop.shape, F32)

    @pl.when(me == blocks - 1)
    def _():
        ybot[...] = jnp.zeros(ybot.shape, F32)

    if rounds > 2:
        pl.semaphore_wait(z_sem.at[2], 2)
    tell(y_sem.at[0], y_near)
    send_left.wait()
    send_right.wait()

    for g in range(groups):
        if g % 2 == 0:
            halo = jnp.where(spot < 3, hl[g // 2], pltpu.roll(hr[g // 2], 3, 1))
        else:
            halo = jnp.where(spot < 3, pltpu.roll(hl[g // 2], 125, 1), hr[g // 2])
        total = jnp.zeros((ROWS, 128), F32)
        for gap, factor in ((1, 45.0), (2, -9.0), (3, 1.0)):
            from_left = (spot >= 3) & (spot < 3 + gap)
            from_right = (spot >= 3 - gap) & (spot < 3)
            total = total - jnp.where(from_left, factor * pltpu.roll(halo, gap, 1), 0.0)
            total = total + jnp.where(from_right, factor * pltpu.roll(halo, 128 - gap, 1), 0.0)
        xs[g] = total

    def top_out(z):
        return pltpu.make_async_remote_copy(
            ytop_s.at[z],
            ytop.at[z],
            yt_send.at[z],
            yt_recv.at[z],
            device_id=(gx, after_me),
            device_id_type=MESH,
        )

    def bottom_out(z):
        return pltpu.make_async_remote_copy(
            ybot_s.at[z],
            ybot.at[z],
            yb_send.at[z],
            yb_recv.at[z],
            device_id=(gx, before_me),
            device_id_type=MESH,
        )

    def flux_of(z):
        offset = lax.rem(z, 4) * 32
        near = [lane[0:8] < 3, lane[0:8] >= 125]
        for tile in range(ROWS // 8):
            band = slice(8 * tile, 8 * tile + 8)
            packed = xs[z // 4, band]
            edge = [
                pltpu.roll(packed, lax.rem(253 - 6 * f - offset, 128), 1) for f in range(FIELDS)
            ]
            for h in range(2):
                cols = slice(128 * h, 128 * h + 128)
                grads = [
                    gr[z, f, band, cols] + jnp.where(near[h], edge[f], 0.0)
                    for f in range(FIELDS)
                ]
                for f in range(FIELDS):
                    flux = jb[f * FIELDS, band] * grads[0]
                    for other in range(1, FIELDS):
                        flux = flux + jb[f * FIELDS + other, band] * grads[other]
                    fresh = section_a * inc[z, f, band, cols] - flux
                    source = st[z, f, band, cols] + section_b * fresh
                    nin[z, f, band, cols] = fresh
                    sx[z, f, band, cols] = source
                    if tile == 0:
                        ybot_s[z, f, :, cols] = source[0:2]
                    if tile == ROWS // 8 - 1:
                        ytop_s[z, f, :, cols] = source[6:8]

    def section(step):
        z = plane_of(step)
        inc_in(z).wait()
        flux_of(z)

        @pl.when(me < blocks - 1)
        def _():
            top_out(z).start()

        @pl.when(me > 0)
        def _():
            bottom_out(z).start()

    pl.loop(0, planes // 2)(section)
    pl.semaphore_wait(y_sem.at[0], 2)
    tell(y_sem.at[1], y_near)
    pl.loop(planes // 2, planes)(section)

    for copy in near_coefs:
        copy.wait()

    sq[...] = jnp.zeros((128, 128), F32)
    sq[0:1, :] = cb[0]
    sq[1:2, :] = cs[...]
    sq[2:3, :] = cb[1]
    turned = sq[...].T
    alpha = turned[0:ROWS]
    beta = turned[ROWS : 2 * ROWS]
    last = ROWS * blocks - 1
    a, b, e, l, u = factors(alpha, beta, row + ROWS * (lane + me - 1), last)
    weight = (1.0 - 2.0 * alpha + 2.0 * beta) * (1.0 / 16.0)

    def own(x):
        return jnp.broadcast_to(x[:, 1:2], x.shape)

    a_o, b_o, e_o, l_o, u_o, weight_o = [own(x) for x in (a, b, e, l, u, weight)]
    over_e = -1.0 / jnp.where(e_o == 0.0, 1.0, e_o)
    over_a = -1.0 / jnp.where(a_o == 0.0, 1.0, a_o)
    rows_a[0] = b_o * over_e
    rows_a[1] = a_o * over_e
    rows_a[2] = b_o * over_a
    rows_a[3] = e_o * over_a
    one = jnp.ones((1, 128), F32)
    nil = jnp.zeros((1, 128), F32)
    prior, now = nil, one
    prior_d, now_d = nil, one
    rows_a[4, 0:1, :] = now
    rows_a[5, ROWS - 1 : ROWS, :] = nil
    rows_a[5, ROWS - 2 : ROWS - 1, :] = now_d
    for j in range(ROWS - 1):
        prior, now = now, rows_a[0, j : j + 1, :] * now + rows_a[1, j : j + 1, :] * prior
        rows_a[4, j + 1 : j + 2, :] = now
        i = ROWS - 2 - j
        prior_d, now_d = (
            now_d,
            rows_a[2, i : i + 1, :] * now_d + rows_a[3, i : i + 1, :] * prior_d,
        )
        if i > 0:
            rows_a[5, i - 1 : i, :] = now_d
    phi_o = rows_a[4]
    psi_o = rows_a[5]
    sl_o = jnp.where(me == 0, 0.0, psi_o / now_d)
    sr_o = phi_o / now
    wr_o = e_o * (
        phi_o * pltpu.roll(psi_o, ROWS - 1, 0) - pltpu.roll(phi_o, ROWS - 1, 0) * psi_o
    )
    wr_o = 1.0 / jnp.where(row == ROWS - 1, 1.0, wr_o)

    def as_row(x):
        return jnp.sum(jnp.where(row == lane, x, 0.0), axis=0, keepdims=True)

    phi_w = as_row(phi_o * wr_o)
    psi_w = as_row(psi_o * wr_o)
    green = jnp.where(row <= lane, phi_o * psi_w, psi_o * phi_w)
    green = jnp.where((row < ROWS - 1) & (lane < ROWS - 1), green, 0.0)
    a_end, b_end, e_end = a_o[31:32], b_o[31:32], e_o[31:32]
    ratio = jnp.where(e_end == 0.0, 0.0, u_o[31:32] / jnp.where(e_end == 0.0, 1.0, e_end))
    bend = ratio * a_end - l_o[31:32]
    tip = (lane[0:1] == ROWS - 1).astype(F32)
    local = green - l_o * pltpu.roll(green, 1, 0) - u_o * pltpu.roll(green, ROWS - 1, 0)
    end_row = bend * green[30:31] - ratio * tip
    local = jnp.where(row == ROWS - 1, end_row, local)
    pair_row = iota((8, 128), 0)
    pair = jnp.where(
        pair_row == 0,
        tip - a_end * green[30:31],
        jnp.where(pair_row == 1, green[0:1], 0.0),
    )
    shaped = jnp.concatenate([local, pair], axis=0) * as_row(weight_o)
    op = 6.0 * shaped
    op = op - 4.0 * (pltpu.roll(shaped, 1, 1) + pltpu.roll(shaped, 127, 1))
    op = op + (pltpu.roll(shaped, 2, 1) + pltpu.roll(shaped, 126, 1))
    wide = iota((40, 128), 1)
    op = jnp.where(
        wide < 34, op, jnp.where((wide >= 38) & (wide < 40), pltpu.roll(op, 40, 1), 0.0)
    )
    op_high = op.astype(BF16).astype(F32)
    op_low = op - op_high
    packed = jnp.where(wide < 32, op_high, 0.0)
    packed = jnp.where((wide >= 32) & (wide < 64), pltpu.roll(op_high, 32, 1), packed)
    packed = jnp.where((wide >= 64) & (wide < 96), pltpu.roll(op_low, 64, 1), packed)
    packed = jnp.where((wide >= 96) & (wide < 104), pltpu.roll(op_high, 64, 1), packed)
    packed = jnp.where((wide >= 104) & (wide < 112), pltpu.roll(op_high, 72, 1), packed)
    packed = jnp.where((wide >= 112) & (wide < 120), pltpu.roll(op_low, 80, 1), packed)
    wmat[...] = packed.astype(BF16)
    idx = iota((16, 128), 0)
    spread = iota((16, 128), 1)
    field_i = idx - jnp.where(idx >= 5, 5, 0) - jnp.where(idx >= 10, 5, 0)
    kind = jnp.where(idx < 5, op[32:33], jnp.where(idx < 10, op[33:34], 0.0))
    inner = jnp.where(spread < 32, kind, 0.0)
    again = inner + pltpu.roll(inner, 32, 1)
    again = again + pltpu.roll(again, 64, 1)
    place = spread & 31
    place_half = spread & 15
    field_h = place_half >> 1
    ends = [jnp.broadcast_to(kind[:, c : c + 1], (16, 128)) for c in (32, 33, 38, 39)]
    even = (spread & 1) == 0
    outer = jnp.where(
        place < 16, jnp.where(even, ends[0], ends[1]), jnp.where(even, ends[2], ends[3])
    )
    outer = jnp.where(field_h == field_i, outer, 0.0)
    again_high = again.astype(BF16).astype(F32)
    outer_high = outer.astype(BF16).astype(F32)
    quarter = spread >> 5
    for part in range(5):
        lane_at = spread + 128 * part
        field_l = jnp.zeros((16, 128), jnp.int32)
        for q in range(4):
            field_l = jnp.where(quarter == q, (4 * part + q) % 5, field_l)
        own_part = jnp.where(lane_at < 320, again_high, again - again_high)
        own_part = jnp.where(field_l == field_i, own_part, 0.0)
        halo_part = jnp.where(lane_at < 544, outer_high, outer - outer_high)
        value = jnp.where(
            lane_at < 480, own_part, jnp.where(lane_at < 576, halo_part, 0.0)
        )
        wpq[:, 128 * part : 128 * part + 128] = value.astype(BF16)

    sl_before = jnp.where(row == 0, jnp.where(me == 0, 0.0, 1.0), pltpu.roll(sl_o, 1, 0))
    sl_after = jnp.where(row >= ROWS - 2, 0.0, pltpu.roll(sl_o, ROWS - 1, 0))
    sr_before = jnp.where(row == 0, 0.0, pltpu.roll(sr_o, 1, 0))
    sr_after = pltpu.roll(sr_o, ROWS - 1, 0)
    spikes[0] = jnp.where(
        row == ROWS - 1, bend * sl_o[30:31], sl_o - l_o * sl_before - u_o * sl_after
    )
    spikes[1] = jnp.where(
        row == ROWS - 1,
        1.0 + ratio * b_end + bend * sr_o[30:31],
        sr_o - l_o * sr_before - u_o * sr_after,
    )

    tags = [a_end * sl_o[30:31], b_end + a_end * sr_o[30:31], e_end, sl_o[0:1], sr_o[0:1]]
    tag = nil
    for i, value in enumerate(tags):
        tag = jnp.where(lane[0:1] == i, value, tag)

    @pl.loop(0, planes)
    def _(z):
        for h in range(2):
            pqs[z, h, MESSAGE - 1 : MESSAGE, :] = tag


    pl.semaphore_wait(y_sem.at[1], 2)

    def pair_out(z, h):
        return pltpu.make_async_remote_copy(
            pqs.at[z, h],
            rbuf.at[me],
            p_send,
            p_recv,
            device_id=(gx, 2 * z + h),
            device_id_type=MESH,
        )

    def pair_own(z, h):
        return pltpu.make_async_copy(pqs.at[z, h], rbuf.at[me], p_recv)

    @pl.loop(0, planes)
    def _(step):
        z = plane_of(step)

        @pl.when(me > 0)
        def _():
            top_out(z).wait_recv()

        @pl.when(me < blocks - 1)
        def _():
            bottom_out(z).wait_recv()

        high, low = split(sx[z].reshape(FIELDS * ROWS, COLS))
        blank = jnp.zeros((6, COLS), F32)
        halo_high, halo_low = split(
            jnp.concatenate(
                [ybot[z, f] for f in range(FIELDS)]
                + [blank]
                + [ytop[z, f] for f in range(FIELDS)]
                + [blank],
                axis=0,
            )
        )
        stack = jnp.concatenate([high, low, high, halo_high, halo_low, halo_high], axis=0)
        out = jnp.dot(wpq[:, 0:576], stack, preferred_element_type=F32)
        for h in range(2):
            pqs[z, h, 0 : 2 * FIELDS, :] = out[0 : 2 * FIELDS, 128 * h : 128 * h + 128]
        for h in range(2):

            @pl.when(2 * z + h == me)
            def _():
                pair_own(z, h).start()

            @pl.when(2 * z + h != me)
            def _():
                pair_out(z, h).start()

    @pl.loop(0, planes)
    def _(z):
        weights = wmat[...]
        gap = jnp.zeros((4, COLS), F32)
        for f in range(FIELDS):
            source = sx[z, f]
            high, low = split(source)
            halo = jnp.concatenate([ybot[z, f], gap, ytop[z, f]], axis=0)
            halo_high = halo.astype(BF16).astype(F32)
            halo_low = halo - halo_high
            halos = jnp.concatenate([halo_high, halo_low], axis=0).astype(BF16)
            again = jnp.concatenate([halo_high, jnp.zeros((8, COLS), F32)], axis=0).astype(BF16)
            stack = jnp.concatenate([high, low, high, halos, again], axis=0)
            out = jnp.dot(weights, stack, preferred_element_type=F32)
            zl[z, f] = source - out[0:ROWS]

    @pl.loop(0, planes)
    def _(z):
        @pl.when(me < blocks - 1)
        def _():
            top_out(z).wait_send()

        @pl.when(me > 0)
        def _():
            bottom_out(z).wait_send()

    pltpu.make_async_copy(rbuf, rbuf, p_recv).wait()

    tagged = jnp.concatenate([rbuf[k, MESSAGE - 1 : MESSAGE, :] for k in range(blocks)], axis=0)
    block = iota((blocks, 128), 0)

    def quantity(i):
        return jnp.broadcast_to(tagged[:, i : i + 1], (blocks, 128))

    def following(x):
        return jnp.where(block == blocks - 1, 0.0, pltpu.roll(x, blocks - 1, 0))

    e_cut = quantity(2)
    low_c = quantity(0)
    mid_c = quantity(1) + e_cut * following(quantity(3))
    up_c = e_cut * following(quantity(4))
    over_up = -1.0 / jnp.where(up_c == 0.0, 1.0, up_c)
    over_low = -1.0 / jnp.where(low_c == 0.0, 1.0, low_c)
    rows_b[0] = low_c * over_up
    rows_b[1] = mid_c * over_up
    rows_b[2] = mid_c * over_low
    rows_b[3] = up_c * over_low
    rows_b[4, 0:1, :] = one
    rows_b[5, blocks - 1 : blocks, :] = one
    prior, now = nil, one
    prior_d, now_d = nil, one
    for k in range(blocks - 1):
        prior, now = now, rows_b[0, k : k + 1, :] * prior + rows_b[1, k : k + 1, :] * now
        rows_b[4, k + 1 : k + 2, :] = now
        i = blocks - 1 - k
        prior_d, now_d = (
            now_d,
            rows_b[2, i : i + 1, :] * now_d + rows_b[3, i : i + 1, :] * prior_d,
        )
        rows_b[5, i - 1 : i, :] = now_d
    phi_b, psi_b = rows_b[4], rows_b[5]
    leading = jnp.where(block == 0, 0.0, pltpu.roll(phi_b, 1, 0))
    turn = low_c * leading + mid_c * phi_b
    scale = 1.0 / (psi_b * turn + up_c * phi_b * following(psi_b))
    rows_b[6] = phi_b * scale
    rows_b[7] = psi_b * scale
    rows_b[8] = e_cut

    right_sides = []
    for k in range(blocks):
        side_k = rbuf[k, 0:FIELDS]
        if k < blocks - 1:
            side_k = side_k - rows_b[8, k : k + 1, :] * rbuf[k + 1, FIELDS : 2 * FIELDS]
        right_sides.append(side_k)
    tail = jnp.zeros((FIELDS, 128), F32)
    for k in range(blocks - 1, -1, -1):
        ss[k + 1] = rows_b[4, k : k + 1, :] * tail
        tail = tail + rows_b[7, k : k + 1, :] * right_sides[k]
    front = jnp.zeros((FIELDS, 128), F32)
    ss[0] = front
    for k in range(blocks):
        front = front + rows_b[6, k : k + 1, :] * right_sides[k]
        ss[k + 1] = ss[k + 1] + rows_b[5, k : k + 1, :] * front

    def sep_out(step):
        k = lax.rem(me + 1 + lax.rem(step + 4, blocks - 1), blocks)
        return pltpu.make_async_remote_copy(
            ss.at[pl.ds(k, 2)],
            sbuf.at[me],
            s_send,
            s_recv,
            device_id=(gx, k),
            device_id_type=MESH,
        )

    @pl.loop(0, blocks - 1)
    def _(step):
        sep_out(step).start()

    pltpu.make_async_copy(ss.at[pl.ds(me, 2)], sbuf.at[me], s_recv).start()

    sent = pl.ds(0, blocks - 1)
    pltpu.make_async_copy(rbuf.at[sent], rbuf.at[sent], p_send).wait()
    pltpu.make_async_copy(sbuf, sbuf, s_recv).wait()
    pltpu.make_async_copy(sbuf.at[sent], sbuf.at[sent], s_send).wait()


def finish(planes, zl, nin, sbuf, spikes, new_state, new_inc, ready, state_sem, inc_sem):
    def inc_out(z):
        return pltpu.make_async_copy(nin.at[z], new_inc.at[:, z], inc_sem.at[z])

    def state_out(z):
        return pltpu.make_async_copy(ready.at[z], new_state.at[:, z], state_sem.at[z])

    @pl.loop(0, planes)
    def _(z):
        inc_out(z).start()

    @pl.loop(0, planes)
    def _(z):
        for h in range(2):
            k = 2 * z + h
            cols = slice(128 * h, 128 * h + 128)
            for f in range(FIELDS):
                under = sbuf[k, 0, f : f + 1, :]
                over = sbuf[k, 1, f : f + 1, :]
                ready[z, f, :, cols] = (
                    zl[z, f, :, cols] - spikes[0] * under - spikes[1] * over
                )
        state_out(z).start()

    @pl.loop(0, planes)
    def _(z):
        state_out(z).wait()
        inc_out(z).wait()


def shards(state, increment, jacobian, filter_alpha, filter_beta):
    fields, planes, rows, cols = state.shape
    blocks = lax.axis_size("gy")
    widths = lax.axis_size("gx")
    groups = planes // 4
    full = (planes, fields, rows, cols)
    halo = (planes, fields, 2, cols)
    dma = pltpu.SemaphoreType.DMA
    anywhere = pl.BlockSpec(memory_space=pltpu.HBM)
    near = pl.BlockSpec(memory_space=pltpu.VMEM)
    whole = jax.ShapeDtypeStruct(state.shape, F32)
    zl, nin, sbuf, spikes = pl.pallas_call(
        functools.partial(kernel, blocks, planes, widths),
        out_shape=(
            jax.ShapeDtypeStruct(full, F32),
            jax.ShapeDtypeStruct(full, F32),
            jax.ShapeDtypeStruct((blocks, 2, fields, 128), F32),
            jax.ShapeDtypeStruct((2, rows, 128), F32),
        ),
        in_specs=[anywhere] * 6,
        out_specs=(near,) * 4,
        scratch_shapes=[
            pltpu.VMEM(full, F32),
            pltpu.VMEM(full, F32),
            pltpu.VMEM(full, F32),
            pltpu.VMEM(full, F32),
            pltpu.VMEM((fields * fields, rows, 128), F32),
            pltpu.VMEM((fields, fields, rows), F32),
            pltpu.VMEM((cols, cols), BF16),
            pltpu.VMEM((groups, rows, 128), F32),
            pltpu.VMEM(((groups + 1) // 2, rows, 128), F32),
            pltpu.VMEM(((groups + 1) // 2, rows, 128), F32),
            pltpu.VMEM(((groups + 1) // 2, rows, 128), F32),
            pltpu.VMEM(((groups + 1) // 2, rows, 128), F32),
            pltpu.VMEM(halo, F32),
            pltpu.VMEM(halo, F32),
            pltpu.VMEM(halo, F32),
            pltpu.VMEM(halo, F32),
            pltpu.VMEM((2, 1, rows), F32),
            pltpu.VMEM((1, 128), F32),
            pltpu.VMEM((2, 1, 128), F32),
            pltpu.VMEM((128, 128), F32),
            pltpu.VMEM((6, rows, 128), F32),
            pltpu.VMEM((9, blocks, 128), F32),
            pltpu.VMEM((16, 640), BF16),
            pltpu.VMEM((planes, 2, MESSAGE, 128), F32),
            pltpu.VMEM((blocks, MESSAGE, 128), F32),
            pltpu.VMEM((blocks + 1, fields, 128), F32),
            pltpu.VMEM((40, 128), BF16),
            dma((planes,)),
            dma((planes,)),
            dma((4,)),
            pltpu.SemaphoreType.REGULAR((3,)),
            pltpu.SemaphoreType.REGULAR((2,)),
            dma((2,)),
            dma((2,)),
            dma((2,)),
            dma((2,)),
            dma((planes,)),
            dma((planes,)),
            dma((planes,)),
            dma((planes,)),
            dma,
            dma,
            dma,
            dma,
        ],
        compiler_params=pltpu.CompilerParams(
            collective_id=0, has_side_effects=True, vmem_limit_bytes=32 * 1024 * 1024
        ),
    )(
        *[
            pltpu.with_memory_space_constraint(x, pltpu.HBM)
            for x in (
                state,
                increment,
                filter_alpha.reshape(1, rows),
                filter_beta.reshape(1, rows),
                jacobian,
                stencil_weights(),
            )
        ]
    )
    return pl.pallas_call(
        functools.partial(finish, planes),
        out_shape=(whole, whole),
        in_specs=[near] * 4,
        out_specs=(anywhere, anywhere),
        scratch_shapes=[pltpu.VMEM(full, F32), dma((planes,)), dma((planes,))],
        compiler_params=pltpu.CompilerParams(vmem_limit_bytes=24 * 1024 * 1024),
    )(zl, nin, sbuf, spikes)


def solution(mesh):
    placed = (
        P(None, None, "gy", "gx"),
        P(None, None, "gy", "gx"),
        P(None, None, "gy"),
        P("gy"),
        P("gy"),
    )
    return jax.shard_map(
        shards,
        mesh=mesh,
        in_specs=placed,
        out_specs=(P(None, None, "gy", "gx"), P(None, None, "gy", "gx")),
        check_vma=False,
    )
```

```python
import functools

import jax
import jax.numpy as jnp
import numpy as np
from jax import lax
from jax.experimental import pallas as pl
from jax.experimental.pallas import tpu as pltpu
from jax.sharding import PartitionSpec as P

section_a = -5.0 / 9.0
section_b = 15.0 / 16.0
courant = 0.5
MESH = pl.DeviceIdType.MESH
F32 = jnp.float32
BF16 = jnp.bfloat16
FIELDS = 5
ROWS = 32
MESSAGE = 10
COLS = 256


def iota(shape, dim):
    return lax.broadcasted_iota(jnp.int32, shape, dim)


def split(x):
    high = x.astype(BF16)
    return high, (x - high.astype(F32)).astype(BF16)


def stencil_weights():
    gap = np.arange(COLS)[:, None] - np.arange(COLS)[None, :]
    size = np.abs(gap)
    weight = np.where(size == 1, 45.0, np.where(size == 2, -9.0, np.where(size == 3, 1.0, 0.0)))
    return jnp.asarray(np.sign(gap) * weight, BF16)


def before(x):
    rolled = pltpu.roll(x, 1, 0)
    return jnp.where(iota(x.shape, 0) == 0, pltpu.roll(rolled, 1, 1), rolled)


def after(x):
    rolled = pltpu.roll(x, ROWS - 1, 0)
    return jnp.where(iota(x.shape, 0) == ROWS - 1, pltpu.roll(rolled, 127, 1), rolled)


def factors(alpha, beta, point, last):
    inner = (point >= 1) & (point < last)
    low_one = jnp.where((point >= 1) & (point <= last), alpha, 0.0)
    up_one = jnp.where(point < last, alpha, 0.0)
    low_two = jnp.where(inner, after(beta), 0.0)
    up_two = jnp.where(inner, before(beta), 0.0)
    a, e, b = low_one, up_one, jnp.ones(alpha.shape, F32)
    for _ in range(3):
        l = low_two / jnp.where(inner, after(a), 1.0)
        u = up_two / jnp.where(inner, before(e), 1.0)
        a = low_one - b * l
        e = up_one - b * u
        b = (
            1.0
            - a * jnp.where(point >= 1, before(u), 0.0)
            - e * jnp.where(point < last, after(l), 0.0)
        )
    return a, b, e, l, u


def kernel(
    blocks,
    planes,
    widths,
    state,
    increment,
    alpha_ref,
    beta_ref,
    jac_ref,
    dxw_ref,
    zl,
    nin,
    sbuf,
    spikes,
    st,
    inc,
    gr,
    sx,
    jb,
    jv,
    dxw,
    xs,
    to_left,
    to_right,
    hl,
    hr,
    ytop_s,
    ybot_s,
    ytop,
    ybot,
    av,
    cs,
    cb,
    sq,
    rows_a,
    rows_b,
    wpq,
    tag_s,
    tags_all,
    pqs,
    rbuf,
    ss,
    wmat,
    st_sem,
    inc_sem,
    in_sem,
    z_sem,
    y_sem,
    x_send,
    x_recv,
    c_send,
    c_recv,
    yt_send,
    yt_recv,
    yb_send,
    yb_recv,
    p_send,
    p_recv,
    s_send,
    s_recv,
    t_send,
    t_recv,
):
    gx = lax.axis_index("gx")
    me = lax.axis_index("gy")
    left = lax.rem(gx + widths - 1, widths)
    right = lax.rem(gx + 1, widths)
    groups = planes // 4
    home = me // 2
    ring = max(blocks // 4, 1)
    sheets = blocks // ring
    rounds = max(ring // 2 - 1, 0)
    gz = lax.rem(me, ring)
    gq = me // ring
    z_near = [gq * ring + lax.rem(gz + move, ring) for move in (1, ring - 1)]
    y_near = [lax.rem(gq + move, sheets) * ring + gz for move in (1, sheets - 1)]
    after_me = lax.rem(me + 1, blocks)
    before_me = lax.rem(me + blocks - 1, blocks)
    lane = iota((ROWS, 128), 1)
    row = iota((ROWS, 128), 0)

    barrier = pltpu.get_barrier_semaphore()
    for peer in [(left, me), (right, me)] + [
        (gx, other) for other in z_near + y_near + [after_me, before_me]
    ]:
        pl.semaphore_signal(barrier, inc=1, device_id=peer, device_id_type=MESH)

    def tell(sem, peers):
        for other in peers:
            pl.semaphore_signal(sem, inc=1, device_id=(gx, other), device_id_type=MESH)

    def plane_of(step):
        return lax.rem(step + home + 2, planes)

    def state_in(z):
        return pltpu.make_async_copy(state.at[:, z], st.at[z], st_sem.at[z])

    def inc_in(z):
        return pltpu.make_async_copy(increment.at[:, z], inc.at[z], inc_sem.at[z])

    small_in = [
        pltpu.make_async_copy(alpha_ref, av.at[0], in_sem.at[0]),
        pltpu.make_async_copy(beta_ref, av.at[1], in_sem.at[1]),
        pltpu.make_async_copy(jac_ref, jv, in_sem.at[2]),
        pltpu.make_async_copy(dxw_ref, dxw, in_sem.at[3]),
    ]
    for copy in small_in:
        copy.start()

    @pl.loop(0, planes)
    def _(z):
        state_in(z).start()

    @pl.loop(0, planes)
    def _(step):
        inc_in(plane_of(step)).start()

    @pl.loop(0, groups)
    def _(g):
        for q in range(4):
            state_in(g * 4 + q).wait()
        edges = jnp.zeros((ROWS, 128), F32)
        for q in range(4):
            z = g * 4 + q
            for f in range(FIELDS):
                base = q * 32 + f * 6
                ends = jnp.where(lane < 64, st[z, f, :, 0:128], st[z, f, :, 128:256])
                moved = pltpu.roll(ends, base + 3, 1)
                edges = jnp.where((lane >= base) & (lane < base + 6), moved, edges)
        xs[g] = edges

    for copy in small_in:
        copy.wait()
    cs[...] = jnp.zeros((1, 128), F32)
    cs[:, 0:ROWS] = av[0]
    cs[:, ROWS : 2 * ROWS] = av[1]

    spot = lax.rem(lax.rem(lane, 32), 6)
    pairs = (groups + 1) // 2
    for p in range(pairs):
        one, two = xs[2 * p], xs[min(2 * p + 1, groups - 1)]
        to_right[p] = jnp.where(spot < 3, one, pltpu.roll(two, 3, 1))
        to_left[p] = jnp.where(spot < 3, pltpu.roll(one, 125, 1), two)

    pl.semaphore_wait(barrier, 8)

    send_left = pltpu.make_async_remote_copy(
        to_left, hr, x_send.at[0], x_recv.at[0], device_id=(left, me), device_id_type=MESH
    )
    send_right = pltpu.make_async_remote_copy(
        to_right, hl, x_send.at[1], x_recv.at[1], device_id=(right, me), device_id_type=MESH
    )
    send_left.start()
    send_right.start()
    if rounds > 0:
        tell(z_sem.at[0], z_near)
    near_coefs = [
        pltpu.make_async_remote_copy(
            cs,
            cb.at[i],
            c_send.at[i],
            c_recv.at[i],
            device_id=(gx, other),
            device_id_type=MESH,
        )
        for i, other in enumerate([after_me, before_me])
    ]
    for copy in near_coefs:
        copy.start()

    sq[...] = jnp.zeros((128, 128), F32)
    for f in range(FIELDS):
        sq[8 * f : 8 * f + FIELDS, 0:ROWS] = jv[f]
    jac_t = sq[...].T
    for f in range(FIELDS):
        for g in range(FIELDS):
            pick = jac_t[0:ROWS, 8 * f + g : 8 * f + g + 1]
            jb[f * FIELDS + g] = jnp.broadcast_to(pick, (ROWS, 128)) * (courant / 60.0)

    def gradient(step):
        z = pl.ds(4 * step, 4)
        high, low = split(st[z].reshape(4 * FIELDS * ROWS, COLS))
        weights = dxw[...]
        total = jnp.dot(high, weights, preferred_element_type=F32) + jnp.dot(
            low, weights, preferred_element_type=F32
        )
        gr[z] = total.reshape(4, FIELDS, ROWS, COLS)

    pl.loop(0, planes // 8)(gradient)
    if rounds > 0:
        pl.semaphore_wait(z_sem.at[0], 2)
    if rounds > 1:
        tell(z_sem.at[1], z_near)
    pl.loop(planes // 8, planes // 4)(gradient)
    if rounds > 1:
        pl.semaphore_wait(z_sem.at[1], 2)
    if rounds > 2:
        tell(z_sem.at[2], z_near)
    @pl.when(me == 0)
    def _():
        ytop[...] = jnp.zeros(ytop.shape, F32)

    @pl.when(me == blocks - 1)
    def _():
        ybot[...] = jnp.zeros(ybot.shape, F32)

    send_left.wait()
    send_right.wait()

    for g in range(groups):
        if g % 2 == 0:
            halo = jnp.where(spot < 3, hl[g // 2], pltpu.roll(hr[g // 2], 3, 1))
        else:
            halo = jnp.where(spot < 3, pltpu.roll(hl[g // 2], 125, 1), hr[g // 2])
        total = jnp.zeros((ROWS, 128), F32)
        for gap, factor in ((1, 45.0), (2, -9.0), (3, 1.0)):
            from_left = (spot >= 3) & (spot < 3 + gap)
            from_right = (spot >= 3 - gap) & (spot < 3)
            total = total - jnp.where(from_left, factor * pltpu.roll(halo, gap, 1), 0.0)
            total = total + jnp.where(from_right, factor * pltpu.roll(halo, 128 - gap, 1), 0.0)
        xs[g] = total

    def top_out(z):
        return pltpu.make_async_remote_copy(
            ytop_s.at[z],
            ytop.at[z],
            yt_send.at[z],
            yt_recv.at[z],
            device_id=(gx, after_me),
            device_id_type=MESH,
        )

    def bottom_out(z):
        return pltpu.make_async_remote_copy(
            ybot_s.at[z],
            ybot.at[z],
            yb_send.at[z],
            yb_recv.at[z],
            device_id=(gx, before_me),
            device_id_type=MESH,
        )

    def flux_of(z):
        offset = lax.rem(z, 4) * 32
        near = [lane[0:8] < 3, lane[0:8] >= 125]
        for tile in range(ROWS // 8):
            band = slice(8 * tile, 8 * tile + 8)
            packed = xs[z // 4, band]
            edge = [
                pltpu.roll(packed, lax.rem(253 - 6 * f - offset, 128), 1) for f in range(FIELDS)
            ]
            halves = [slice(0, 128), slice(128, 256)]
            grads = [
                [
                    gr[z, f, band, halves[h]] + jnp.where(near[h], edge[f], 0.0)
                    for f in range(FIELDS)
                ]
                for h in range(2)
            ]
            for f in range(FIELDS):
                slopes = [jb[f * FIELDS + other, band] for other in range(FIELDS)]
                for h in range(2):
                    cols = halves[h]
                    flux = slopes[0] * grads[h][0]
                    for other in range(1, FIELDS):
                        flux = flux + slopes[other] * grads[h][other]
                    fresh = section_a * inc[z, f, band, cols] - flux
                    source = st[z, f, band, cols] + section_b * fresh
                    nin[z, f, band, cols] = fresh
                    sx[z, f, band, cols] = source
                    if tile == 0:
                        ybot_s[z, f, :, cols] = source[0:2]
                    if tile == ROWS // 8 - 1:
                        ytop_s[z, f, :, cols] = source[6:8]

    def section(step):
        z = plane_of(step)
        inc_in(z).wait()
        flux_of(z)

        @pl.when(me < blocks - 1)
        def _():
            top_out(z).start()

        @pl.when(me > 0)
        def _():
            bottom_out(z).start()

    pl.loop(0, planes // 2)(section)
    if rounds > 2:
        pl.semaphore_wait(z_sem.at[2], 2)
    tell(y_sem.at[0], y_near)
    pl.loop(planes // 2, planes)(section)
    pl.semaphore_wait(y_sem.at[0], 2)
    tell(y_sem.at[1], y_near)

    for copy in near_coefs:
        copy.wait()

    sq[...] = jnp.zeros((128, 128), F32)
    sq[0:1, :] = cb[0]
    sq[1:2, :] = cs[...]
    sq[2:3, :] = cb[1]
    turned = sq[...].T
    alpha = turned[0:ROWS]
    beta = turned[ROWS : 2 * ROWS]
    last = ROWS * blocks - 1
    a, b, e, l, u = factors(alpha, beta, row + ROWS * (lane + me - 1), last)
    weight = (1.0 - 2.0 * alpha + 2.0 * beta) * (1.0 / 16.0)

    def own(x):
        return jnp.broadcast_to(x[:, 1:2], x.shape)

    a_o, b_o, e_o, l_o, u_o, weight_o = [own(x) for x in (a, b, e, l, u, weight)]
    over_e = -1.0 / jnp.where(e_o == 0.0, 1.0, e_o)
    over_a = -1.0 / jnp.where(a_o == 0.0, 1.0, a_o)
    rows_a[0] = b_o * over_e
    rows_a[1] = a_o * over_e
    rows_a[2] = b_o * over_a
    rows_a[3] = e_o * over_a
    one = jnp.ones((1, 128), F32)
    nil = jnp.zeros((1, 128), F32)
    prior, now = nil, one
    prior_d, now_d = nil, one
    rows_a[4, 0:1, :] = now
    rows_a[5, ROWS - 1 : ROWS, :] = nil
    rows_a[5, ROWS - 2 : ROWS - 1, :] = now_d
    for j in range(ROWS - 1):
        prior, now = now, rows_a[0, j : j + 1, :] * now + rows_a[1, j : j + 1, :] * prior
        rows_a[4, j + 1 : j + 2, :] = now
        i = ROWS - 2 - j
        prior_d, now_d = (
            now_d,
            rows_a[2, i : i + 1, :] * now_d + rows_a[3, i : i + 1, :] * prior_d,
        )
        if i > 0:
            rows_a[5, i - 1 : i, :] = now_d
    phi_o = rows_a[4]
    psi_o = rows_a[5]
    sl_o = jnp.where(me == 0, 0.0, psi_o / now_d)
    sr_o = phi_o / now
    wr_o = e_o * (
        phi_o * pltpu.roll(psi_o, ROWS - 1, 0) - pltpu.roll(phi_o, ROWS - 1, 0) * psi_o
    )
    wr_o = 1.0 / jnp.where(row == ROWS - 1, 1.0, wr_o)

    def as_row(x):
        return jnp.sum(jnp.where(row == lane, x, 0.0), axis=0, keepdims=True)

    phi_w = as_row(phi_o * wr_o)
    psi_w = as_row(psi_o * wr_o)
    green = jnp.where(row <= lane, phi_o * psi_w, psi_o * phi_w)
    green = jnp.where((row < ROWS - 1) & (lane < ROWS - 1), green, 0.0)
    a_end, b_end, e_end = a_o[31:32], b_o[31:32], e_o[31:32]
    ratio = jnp.where(e_end == 0.0, 0.0, u_o[31:32] / jnp.where(e_end == 0.0, 1.0, e_end))
    bend = ratio * a_end - l_o[31:32]
    tip = (lane[0:1] == ROWS - 1).astype(F32)
    local = green - l_o * pltpu.roll(green, 1, 0) - u_o * pltpu.roll(green, ROWS - 1, 0)
    end_row = bend * green[30:31] - ratio * tip
    local = jnp.where(row == ROWS - 1, end_row, local)
    pair_row = iota((8, 128), 0)
    pair = jnp.where(
        pair_row == 0,
        tip - a_end * green[30:31],
        jnp.where(pair_row == 1, green[0:1], 0.0),
    )
    shaped = jnp.concatenate([local, pair], axis=0) * as_row(weight_o)
    op = 6.0 * shaped
    op = op - 4.0 * (pltpu.roll(shaped, 1, 1) + pltpu.roll(shaped, 127, 1))
    op = op + (pltpu.roll(shaped, 2, 1) + pltpu.roll(shaped, 126, 1))
    wide = iota((40, 128), 1)
    op = jnp.where(
        wide < 34, op, jnp.where((wide >= 38) & (wide < 40), pltpu.roll(op, 40, 1), 0.0)
    )
    op_high = op.astype(BF16).astype(F32)
    op_low = op - op_high
    packed = jnp.where(wide < 32, op_high, 0.0)
    packed = jnp.where((wide >= 32) & (wide < 64), pltpu.roll(op_high, 32, 1), packed)
    packed = jnp.where((wide >= 64) & (wide < 96), pltpu.roll(op_low, 64, 1), packed)
    packed = jnp.where((wide >= 96) & (wide < 104), pltpu.roll(op_high, 64, 1), packed)
    packed = jnp.where((wide >= 104) & (wide < 112), pltpu.roll(op_high, 72, 1), packed)
    packed = jnp.where((wide >= 112) & (wide < 120), pltpu.roll(op_low, 80, 1), packed)
    wmat[...] = packed.astype(BF16)
    idx = iota((16, 128), 0)
    spread = iota((16, 128), 1)
    field_i = idx - jnp.where(idx >= 5, 5, 0) - jnp.where(idx >= 10, 5, 0)
    kind = jnp.where(idx < 5, op[32:33], jnp.where(idx < 10, op[33:34], 0.0))
    inner = jnp.where(spread < 32, kind, 0.0)
    again = inner + pltpu.roll(inner, 32, 1)
    again = again + pltpu.roll(again, 64, 1)
    place = spread & 31
    place_half = spread & 15
    field_h = place_half >> 1
    ends = [jnp.broadcast_to(kind[:, c : c + 1], (16, 128)) for c in (32, 33, 38, 39)]
    even = (spread & 1) == 0
    outer = jnp.where(
        place < 16, jnp.where(even, ends[0], ends[1]), jnp.where(even, ends[2], ends[3])
    )
    outer = jnp.where(field_h == field_i, outer, 0.0)
    again_high = again.astype(BF16).astype(F32)
    outer_high = outer.astype(BF16).astype(F32)
    quarter = spread >> 5
    for part in range(5):
        lane_at = spread + 128 * part
        field_l = jnp.zeros((16, 128), jnp.int32)
        for q in range(4):
            field_l = jnp.where(quarter == q, (4 * part + q) % 5, field_l)
        own_part = jnp.where(lane_at < 320, again_high, again - again_high)
        own_part = jnp.where(field_l == field_i, own_part, 0.0)
        halo_part = jnp.where(lane_at < 544, outer_high, outer - outer_high)
        value = jnp.where(
            lane_at < 480, own_part, jnp.where(lane_at < 576, halo_part, 0.0)
        )
        wpq[:, 128 * part : 128 * part + 128] = value.astype(BF16)

    sl_before = jnp.where(row == 0, jnp.where(me == 0, 0.0, 1.0), pltpu.roll(sl_o, 1, 0))
    sl_after = jnp.where(row >= ROWS - 2, 0.0, pltpu.roll(sl_o, ROWS - 1, 0))
    sr_before = jnp.where(row == 0, 0.0, pltpu.roll(sr_o, 1, 0))
    sr_after = pltpu.roll(sr_o, ROWS - 1, 0)
    spikes[0] = jnp.where(
        row == ROWS - 1, bend * sl_o[30:31], sl_o - l_o * sl_before - u_o * sl_after
    )
    spikes[1] = jnp.where(
        row == ROWS - 1,
        1.0 + ratio * b_end + bend * sr_o[30:31],
        sr_o - l_o * sr_before - u_o * sr_after,
    )

    tags = [a_end * sl_o[30:31], b_end + a_end * sr_o[30:31], e_end, sl_o[0:1], sr_o[0:1]]
    tag = nil
    for i, value in enumerate(tags):
        tag = jnp.where(lane[0:1] == i, value, tag)

    tag_s[...] = tag


    pl.semaphore_wait(y_sem.at[1], 2)

    def tag_out(step):
        return pltpu.make_async_remote_copy(
            tag_s,
            tags_all.at[me],
            t_send,
            t_recv,
            device_id=(gx, lax.rem(me + 1 + (step + 4) % (blocks - 1), blocks)),
            device_id_type=MESH,
        )

    for step in range(blocks - 1):
        tag_out(step).start()
    pltpu.make_async_copy(tag_s, tags_all.at[me], t_recv).start()

    def pair_out(z, h):
        return pltpu.make_async_remote_copy(
            pqs.at[z, h],
            rbuf.at[me],
            p_send,
            p_recv,
            device_id=(gx, 2 * z + h),
            device_id_type=MESH,
        )

    def pair_own(z, h):
        return pltpu.make_async_copy(pqs.at[z, h], rbuf.at[me], p_recv)

    def messages(step, holds_own):
        pair = [plane_of(2 * step), plane_of(2 * step + 1)]

        @pl.when(me > 0)
        def _():
            for z in pair:
                top_out(z).wait_recv()

        @pl.when(me < blocks - 1)
        def _():
            for z in pair:
                bottom_out(z).wait_recv()

        for z in pair:
            high, low = split(sx[z].reshape(FIELDS * ROWS, COLS))
            blank = jnp.zeros((6, COLS), F32)
            halo_high, halo_low = split(
                jnp.concatenate(
                    [ybot[z, f] for f in range(FIELDS)]
                    + [blank]
                    + [ytop[z, f] for f in range(FIELDS)]
                    + [blank],
                    axis=0,
                )
            )
            stack = jnp.concatenate([high, low, high, halo_high, halo_low, halo_high], axis=0)
            out = jnp.dot(wpq[:, 0:576], stack, preferred_element_type=F32)
            for h in range(2):
                pqs[z, h, 0 : 2 * FIELDS, :] = out[0 : 2 * FIELDS, 128 * h : 128 * h + 128]
        for i, z in enumerate(pair):
            for h in range(2):
                if holds_own and i == 0:

                    @pl.when(2 * z + h == me)
                    def _():
                        pair_own(z, h).start()

                    @pl.when(2 * z + h != me)
                    def _():
                        pair_out(z, h).start()

                else:
                    pair_out(z, h).start()

    @pl.loop(0, planes // 2 - 1)
    def _(step):
        messages(step, False)

    messages(planes // 2 - 1, True)

    pltpu.make_async_copy(tags_all, tags_all, t_recv).wait()

    tagged = jnp.concatenate([tags_all[k] for k in range(blocks)], axis=0)
    block = iota((blocks, 128), 0)

    def quantity(i):
        return jnp.broadcast_to(tagged[:, i : i + 1], (blocks, 128))

    def following(x):
        return jnp.where(block == blocks - 1, 0.0, pltpu.roll(x, blocks - 1, 0))

    e_cut = quantity(2)
    low_c = quantity(0)
    mid_c = quantity(1) + e_cut * following(quantity(3))
    up_c = e_cut * following(quantity(4))
    over_up = -1.0 / jnp.where(up_c == 0.0, 1.0, up_c)
    over_low = -1.0 / jnp.where(low_c == 0.0, 1.0, low_c)
    rows_b[0] = low_c * over_up
    rows_b[1] = mid_c * over_up
    rows_b[2] = mid_c * over_low
    rows_b[3] = up_c * over_low
    rows_b[4, 0:1, :] = one
    rows_b[5, blocks - 1 : blocks, :] = one
    prior, now = nil, one
    prior_d, now_d = nil, one
    for k in range(blocks - 1):
        prior, now = now, rows_b[0, k : k + 1, :] * prior + rows_b[1, k : k + 1, :] * now
        rows_b[4, k + 1 : k + 2, :] = now
        i = blocks - 1 - k
        prior_d, now_d = (
            now_d,
            rows_b[2, i : i + 1, :] * now_d + rows_b[3, i : i + 1, :] * prior_d,
        )
        rows_b[5, i - 1 : i, :] = now_d
    phi_b, psi_b = rows_b[4], rows_b[5]
    leading = jnp.where(block == 0, 0.0, pltpu.roll(phi_b, 1, 0))
    turn = low_c * leading + mid_c * phi_b
    scale = 1.0 / (psi_b * turn + up_c * phi_b * following(psi_b))
    rows_b[6] = phi_b * scale
    rows_b[7] = psi_b * scale
    rows_b[8] = e_cut

    pltpu.make_async_copy(rbuf, rbuf, p_recv).wait()

    right_sides = []
    for k in range(blocks):
        side_k = rbuf[k, 0:FIELDS]
        if k < blocks - 1:
            side_k = side_k - rows_b[8, k : k + 1, :] * rbuf[k + 1, FIELDS : 2 * FIELDS]
        right_sides.append(side_k)
    tail = jnp.zeros((FIELDS, 128), F32)
    for k in range(blocks - 1, -1, -1):
        ss[k + 1] = rows_b[4, k : k + 1, :] * tail
        tail = tail + rows_b[7, k : k + 1, :] * right_sides[k]
    front = jnp.zeros((FIELDS, 128), F32)
    ss[0] = front
    for k in range(blocks):
        front = front + rows_b[6, k : k + 1, :] * right_sides[k]
        ss[k + 1] = ss[k + 1] + rows_b[5, k : k + 1, :] * front

    def sep_out(step):
        k = lax.rem(me + 1 + (step + 4) % (blocks - 1), blocks)
        return pltpu.make_async_remote_copy(
            ss.at[pl.ds(k, 2)],
            sbuf.at[me],
            s_send,
            s_recv,
            device_id=(gx, k),
            device_id_type=MESH,
        )

    for step in range(blocks - 1):
        sep_out(step).start()

    pltpu.make_async_copy(ss.at[pl.ds(me, 2)], sbuf.at[me], s_recv).start()

    @pl.loop(0, planes)
    def _(z):
        weights = wmat[...]
        gap = jnp.zeros((4, COLS), F32)
        for f in range(FIELDS):
            source = sx[z, f]
            high, low = split(source)
            halo = jnp.concatenate([ybot[z, f], gap, ytop[z, f]], axis=0)
            halo_high = halo.astype(BF16).astype(F32)
            halo_low = halo - halo_high
            halos = jnp.concatenate([halo_high, halo_low], axis=0).astype(BF16)
            again = jnp.concatenate([halo_high, jnp.zeros((8, COLS), F32)], axis=0).astype(BF16)
            stack = jnp.concatenate([high, low, high, halos, again], axis=0)
            out = jnp.dot(weights, stack, preferred_element_type=F32)
            zl[z, f] = source - out[0:ROWS]

    @pl.loop(0, planes)
    def _(z):
        @pl.when(me < blocks - 1)
        def _():
            top_out(z).wait_send()

        @pl.when(me > 0)
        def _():
            bottom_out(z).wait_send()

    sent = pl.ds(0, blocks - 1)
    pltpu.make_async_copy(rbuf.at[sent], rbuf.at[sent], p_send).wait()
    pltpu.make_async_copy(tags_all.at[sent], tags_all.at[sent], t_send).wait()
    pltpu.make_async_copy(sbuf, sbuf, s_recv).wait()
    pltpu.make_async_copy(sbuf.at[sent], sbuf.at[sent], s_send).wait()


def finish(planes, zl, nin, sbuf, spikes, new_state, new_inc, ready, state_sem, inc_sem):
    def inc_out(z):
        return pltpu.make_async_copy(nin.at[z], new_inc.at[:, z], inc_sem.at[z])

    def state_out(z):
        return pltpu.make_async_copy(ready.at[z], new_state.at[:, z], state_sem.at[z])

    @pl.loop(0, planes)
    def _(z):
        inc_out(z).start()

    @pl.loop(0, planes)
    def _(z):
        for h in range(2):
            k = 2 * z + h
            cols = slice(128 * h, 128 * h + 128)
            for f in range(FIELDS):
                under = sbuf[k, 0, f : f + 1, :]
                over = sbuf[k, 1, f : f + 1, :]
                ready[z, f, :, cols] = (
                    zl[z, f, :, cols] - spikes[0] * under - spikes[1] * over
                )
        state_out(z).start()

    @pl.loop(0, planes)
    def _(z):
        state_out(z).wait()
        inc_out(z).wait()


def shards(state, increment, jacobian, filter_alpha, filter_beta):
    fields, planes, rows, cols = state.shape
    blocks = lax.axis_size("gy")
    widths = lax.axis_size("gx")
    groups = planes // 4
    full = (planes, fields, rows, cols)
    halo = (planes, fields, 2, cols)
    dma = pltpu.SemaphoreType.DMA
    anywhere = pl.BlockSpec(memory_space=pltpu.HBM)
    near = pl.BlockSpec(memory_space=pltpu.VMEM)
    whole = jax.ShapeDtypeStruct(state.shape, F32)
    zl, nin, sbuf, spikes = pl.pallas_call(
        functools.partial(kernel, blocks, planes, widths),
        out_shape=(
            jax.ShapeDtypeStruct(full, F32),
            jax.ShapeDtypeStruct(full, F32),
            jax.ShapeDtypeStruct((blocks, 2, fields, 128), F32),
            jax.ShapeDtypeStruct((2, rows, 128), F32),
        ),
        in_specs=[anywhere] * 6,
        out_specs=(near,) * 4,
        scratch_shapes=[
            pltpu.VMEM(full, F32),
            pltpu.VMEM(full, F32),
            pltpu.VMEM(full, F32),
            pltpu.VMEM(full, F32),
            pltpu.VMEM((fields * fields, rows, 128), F32),
            pltpu.VMEM((fields, fields, rows), F32),
            pltpu.VMEM((cols, cols), BF16),
            pltpu.VMEM((groups, rows, 128), F32),
            pltpu.VMEM(((groups + 1) // 2, rows, 128), F32),
            pltpu.VMEM(((groups + 1) // 2, rows, 128), F32),
            pltpu.VMEM(((groups + 1) // 2, rows, 128), F32),
            pltpu.VMEM(((groups + 1) // 2, rows, 128), F32),
            pltpu.VMEM(halo, F32),
            pltpu.VMEM(halo, F32),
            pltpu.VMEM(halo, F32),
            pltpu.VMEM(halo, F32),
            pltpu.VMEM((2, 1, rows), F32),
            pltpu.VMEM((1, 128), F32),
            pltpu.VMEM((2, 1, 128), F32),
            pltpu.VMEM((128, 128), F32),
            pltpu.VMEM((6, rows, 128), F32),
            pltpu.VMEM((9, blocks, 128), F32),
            pltpu.VMEM((16, 640), BF16),
            pltpu.VMEM((1, 128), F32),
            pltpu.VMEM((blocks, 1, 128), F32),
            pltpu.VMEM((planes, 2, MESSAGE, 128), F32),
            pltpu.VMEM((blocks, MESSAGE, 128), F32),
            pltpu.VMEM((blocks + 1, fields, 128), F32),
            pltpu.VMEM((40, 128), BF16),
            dma((planes,)),
            dma((planes,)),
            dma((4,)),
            pltpu.SemaphoreType.REGULAR((3,)),
            pltpu.SemaphoreType.REGULAR((2,)),
            dma((2,)),
            dma((2,)),
            dma((2,)),
            dma((2,)),
            dma((planes,)),
            dma((planes,)),
            dma((planes,)),
            dma((planes,)),
            dma,
            dma,
            dma,
            dma,
            dma,
            dma,
        ],
        compiler_params=pltpu.CompilerParams(
            collective_id=0, has_side_effects=True, vmem_limit_bytes=32 * 1024 * 1024
        ),
    )(
        *[
            pltpu.with_memory_space_constraint(x, pltpu.HBM)
            for x in (
                state,
                increment,
                filter_alpha.reshape(1, rows),
                filter_beta.reshape(1, rows),
                jacobian,
                stencil_weights(),
            )
        ]
    )
    return pl.pallas_call(
        functools.partial(finish, planes),
        out_shape=(whole, whole),
        in_specs=[near] * 4,
        out_specs=(anywhere, anywhere),
        scratch_shapes=[pltpu.VMEM(full, F32), dma((planes,)), dma((planes,))],
        compiler_params=pltpu.CompilerParams(vmem_limit_bytes=24 * 1024 * 1024),
    )(zl, nin, sbuf, spikes)


def solution(mesh):
    placed = (
        P(None, None, "gy", "gx"),
        P(None, None, "gy", "gx"),
        P(None, None, "gy"),
        P("gy"),
        P("gy"),
    )
    return jax.shard_map(
        shards,
        mesh=mesh,
        in_specs=placed,
        out_specs=(P(None, None, "gy", "gx"), P(None, None, "gy", "gx")),
        check_vma=False,
    )
```

```python
import functools

import jax
import jax.numpy as jnp
import numpy as np
from jax import lax
from jax.experimental import pallas as pl
from jax.experimental.pallas import tpu as pltpu
from jax.sharding import PartitionSpec as P

section_a = -5.0 / 9.0
section_b = 15.0 / 16.0
courant = 0.5
MESH = pl.DeviceIdType.MESH
F32 = jnp.float32
BF16 = jnp.bfloat16
FIELDS = 5
ROWS = 32
MESSAGE = 10
COLS = 256


def iota(shape, dim):
    return lax.broadcasted_iota(jnp.int32, shape, dim)


def split(x):
    high = x.astype(BF16)
    return high, (x - high.astype(F32)).astype(BF16)


def stencil_weights():
    gap = np.arange(COLS)[:, None] - np.arange(COLS)[None, :]
    size = np.abs(gap)
    weight = np.where(size == 1, 45.0, np.where(size == 2, -9.0, np.where(size == 3, 1.0, 0.0)))
    return jnp.asarray(np.sign(gap) * weight, BF16)


def before(x):
    rolled = pltpu.roll(x, 1, 0)
    return jnp.where(iota(x.shape, 0) == 0, pltpu.roll(rolled, 1, 1), rolled)


def after(x):
    rolled = pltpu.roll(x, ROWS - 1, 0)
    return jnp.where(iota(x.shape, 0) == ROWS - 1, pltpu.roll(rolled, 127, 1), rolled)


def factors(alpha, beta, point, last):
    inner = (point >= 1) & (point < last)
    low_one = jnp.where((point >= 1) & (point <= last), alpha, 0.0)
    up_one = jnp.where(point < last, alpha, 0.0)
    low_two = jnp.where(inner, after(beta), 0.0)
    up_two = jnp.where(inner, before(beta), 0.0)
    a, e, b = low_one, up_one, jnp.ones(alpha.shape, F32)
    for _ in range(3):
        l = low_two / jnp.where(inner, after(a), 1.0)
        u = up_two / jnp.where(inner, before(e), 1.0)
        a = low_one - b * l
        e = up_one - b * u
        b = (
            1.0
            - a * jnp.where(point >= 1, before(u), 0.0)
            - e * jnp.where(point < last, after(l), 0.0)
        )
    return a, b, e, l, u


def kernel(
    blocks,
    planes,
    widths,
    state,
    increment,
    alpha_ref,
    beta_ref,
    jac_ref,
    dxw_ref,
    zl,
    nin,
    sbuf,
    spikes,
    st,
    inc,
    gr,
    sx,
    jb,
    jv,
    dxw,
    xs,
    to_left,
    to_right,
    hl,
    hr,
    ytop_s,
    ybot_s,
    ytop,
    ybot,
    av,
    cs,
    cb,
    sq,
    rows_a,
    rows_b,
    wpq,
    tag_s,
    tags_all,
    pqs,
    rbuf,
    ss,
    wmat,
    st_sem,
    inc_sem,
    in_sem,
    z_sem,
    y_sem,
    x_send,
    x_recv,
    c_send,
    c_recv,
    yt_send,
    yt_recv,
    yb_send,
    yb_recv,
    p_send,
    p_recv,
    s_send,
    s_recv,
    t_send,
    t_recv,
):
    gx = lax.axis_index("gx")
    me = lax.axis_index("gy")
    left = lax.rem(gx + widths - 1, widths)
    right = lax.rem(gx + 1, widths)
    groups = planes // 4
    home = me // 2
    ring = max(blocks // 4, 1)
    sheets = blocks // ring
    rounds = max(ring // 2 - 1, 0)
    gz = lax.rem(me, ring)
    gq = me // ring
    z_near = [gq * ring + lax.rem(gz + move, ring) for move in (1, ring - 1)]
    y_near = [lax.rem(gq + move, sheets) * ring + gz for move in (1, sheets - 1)]
    after_me = lax.rem(me + 1, blocks)
    before_me = lax.rem(me + blocks - 1, blocks)
    lane = iota((ROWS, 128), 1)
    row = iota((ROWS, 128), 0)

    barrier = pltpu.get_barrier_semaphore()
    for peer in [(left, me), (right, me)] + [
        (gx, other) for other in z_near + y_near + [after_me, before_me]
    ]:
        pl.semaphore_signal(barrier, inc=1, device_id=peer, device_id_type=MESH)

    def tell(sem, peers):
        for other in peers:
            pl.semaphore_signal(sem, inc=1, device_id=(gx, other), device_id_type=MESH)

    def plane_of(step):
        return lax.rem(step + home + 2, planes)

    def state_in(z):
        return pltpu.make_async_copy(state.at[:, z], st.at[z], st_sem.at[z])

    def inc_in(z):
        return pltpu.make_async_copy(increment.at[:, z], inc.at[z], inc_sem.at[z])

    small_in = [
        pltpu.make_async_copy(alpha_ref, av.at[0], in_sem.at[0]),
        pltpu.make_async_copy(beta_ref, av.at[1], in_sem.at[1]),
        pltpu.make_async_copy(jac_ref, jv, in_sem.at[2]),
        pltpu.make_async_copy(dxw_ref, dxw, in_sem.at[3]),
    ]
    for copy in small_in:
        copy.start()

    @pl.loop(0, planes)
    def _(z):
        state_in(z).start()

    @pl.loop(0, planes)
    def _(step):
        inc_in(plane_of(step)).start()

    @pl.loop(0, groups)
    def _(g):
        for q in range(4):
            state_in(g * 4 + q).wait()
        edges = jnp.zeros((ROWS, 128), F32)
        for q in range(4):
            z = g * 4 + q
            for f in range(FIELDS):
                base = q * 32 + f * 6
                ends = jnp.where(lane < 64, st[z, f, :, 0:128], st[z, f, :, 128:256])
                moved = pltpu.roll(ends, base + 3, 1)
                edges = jnp.where((lane >= base) & (lane < base + 6), moved, edges)
        xs[g] = edges

    for copy in small_in:
        copy.wait()
    cs[...] = jnp.zeros((1, 128), F32)
    cs[:, 0:ROWS] = av[0]
    cs[:, ROWS : 2 * ROWS] = av[1]

    spot = lax.rem(lax.rem(lane, 32), 6)
    pairs = (groups + 1) // 2
    for p in range(pairs):
        one, two = xs[2 * p], xs[min(2 * p + 1, groups - 1)]
        to_right[p] = jnp.where(spot < 3, one, pltpu.roll(two, 3, 1))
        to_left[p] = jnp.where(spot < 3, pltpu.roll(one, 125, 1), two)

    pl.semaphore_wait(barrier, 8)

    send_left = pltpu.make_async_remote_copy(
        to_left, hr, x_send.at[0], x_recv.at[0], device_id=(left, me), device_id_type=MESH
    )
    send_right = pltpu.make_async_remote_copy(
        to_right, hl, x_send.at[1], x_recv.at[1], device_id=(right, me), device_id_type=MESH
    )
    send_left.start()
    send_right.start()
    if rounds > 0:
        tell(z_sem.at[0], z_near)
    near_coefs = [
        pltpu.make_async_remote_copy(
            cs,
            cb.at[i],
            c_send.at[i],
            c_recv.at[i],
            device_id=(gx, other),
            device_id_type=MESH,
        )
        for i, other in enumerate([after_me, before_me])
    ]
    for copy in near_coefs:
        copy.start()

    sq[...] = jnp.zeros((128, 128), F32)
    for f in range(FIELDS):
        sq[8 * f : 8 * f + FIELDS, 0:ROWS] = jv[f]
    jac_t = sq[...].T
    for f in range(FIELDS):
        for g in range(FIELDS):
            pick = jac_t[0:ROWS, 8 * f + g : 8 * f + g + 1]
            jb[f * FIELDS + g] = jnp.broadcast_to(pick, (ROWS, 128)) * (courant / 60.0)

    def gradient(step):
        z = pl.ds(4 * step, 4)
        high, low = split(st[z].reshape(4 * FIELDS * ROWS, COLS))
        weights = dxw[...]
        total = jnp.dot(high, weights, preferred_element_type=F32) + jnp.dot(
            low, weights, preferred_element_type=F32
        )
        gr[z] = total.reshape(4, FIELDS, ROWS, COLS)

    pl.loop(0, planes // 8)(gradient)
    if rounds > 0:
        pl.semaphore_wait(z_sem.at[0], 2)
    if rounds > 1:
        tell(z_sem.at[1], z_near)
    pl.loop(planes // 8, planes // 4)(gradient)
    if rounds > 1:
        pl.semaphore_wait(z_sem.at[1], 2)
    if rounds > 2:
        tell(z_sem.at[2], z_near)
    @pl.when(me == 0)
    def _():
        ytop[...] = jnp.zeros(ytop.shape, F32)

    @pl.when(me == blocks - 1)
    def _():
        ybot[...] = jnp.zeros(ybot.shape, F32)

    send_left.wait()
    send_right.wait()

    for g in range(groups):
        if g % 2 == 0:
            halo = jnp.where(spot < 3, hl[g // 2], pltpu.roll(hr[g // 2], 3, 1))
        else:
            halo = jnp.where(spot < 3, pltpu.roll(hl[g // 2], 125, 1), hr[g // 2])
        total = jnp.zeros((ROWS, 128), F32)
        for gap, factor in ((1, 45.0), (2, -9.0), (3, 1.0)):
            from_left = (spot >= 3) & (spot < 3 + gap)
            from_right = (spot >= 3 - gap) & (spot < 3)
            total = total - jnp.where(from_left, factor * pltpu.roll(halo, gap, 1), 0.0)
            total = total + jnp.where(from_right, factor * pltpu.roll(halo, 128 - gap, 1), 0.0)
        xs[g] = total

    def top_out(z):
        return pltpu.make_async_remote_copy(
            ytop_s.at[z],
            ytop.at[z],
            yt_send.at[z],
            yt_recv.at[z],
            device_id=(gx, after_me),
            device_id_type=MESH,
        )

    def bottom_out(z):
        return pltpu.make_async_remote_copy(
            ybot_s.at[z],
            ybot.at[z],
            yb_send.at[z],
            yb_recv.at[z],
            device_id=(gx, before_me),
            device_id_type=MESH,
        )

    def flux_of(z):
        offset = lax.rem(z, 4) * 32
        near = [lane[0:8] < 3, lane[0:8] >= 125]
        for tile in range(ROWS // 8):
            band = slice(8 * tile, 8 * tile + 8)
            packed = xs[z // 4, band]
            edge = [
                pltpu.roll(packed, lax.rem(253 - 6 * f - offset, 128), 1) for f in range(FIELDS)
            ]
            halves = [slice(0, 128), slice(128, 256)]
            grads = [
                [
                    gr[z, f, band, halves[h]] + jnp.where(near[h], edge[f], 0.0)
                    for f in range(FIELDS)
                ]
                for h in range(2)
            ]
            for f in range(FIELDS):
                slopes = [jb[f * FIELDS + other, band] for other in range(FIELDS)]
                for h in range(2):
                    cols = halves[h]
                    flux = slopes[0] * grads[h][0]
                    for other in range(1, FIELDS):
                        flux = flux + slopes[other] * grads[h][other]
                    fresh = section_a * inc[z, f, band, cols] - flux
                    source = st[z, f, band, cols] + section_b * fresh
                    nin[z, f, band, cols] = fresh
                    sx[z, f, band, cols] = source
                    if tile == 0:
                        ybot_s[z, f, :, cols] = source[0:2]
                    if tile == ROWS // 8 - 1:
                        ytop_s[z, f, :, cols] = source[6:8]

    def section(step):
        z = plane_of(step)
        inc_in(z).wait()
        flux_of(z)

        @pl.when(me < blocks - 1)
        def _():
            top_out(z).start()

        @pl.when(me > 0)
        def _():
            bottom_out(z).start()

    pl.loop(0, planes // 2)(section)
    if rounds > 2:
        pl.semaphore_wait(z_sem.at[2], 2)
    tell(y_sem.at[0], y_near)
    pl.loop(planes // 2, planes)(section)
    pl.semaphore_wait(y_sem.at[0], 2)
    tell(y_sem.at[1], y_near)

    for copy in near_coefs:
        copy.wait()

    sq[...] = jnp.zeros((128, 128), F32)
    sq[0:1, :] = cb[0]
    sq[1:2, :] = cs[...]
    sq[2:3, :] = cb[1]
    turned = sq[...].T
    alpha = turned[0:ROWS]
    beta = turned[ROWS : 2 * ROWS]
    last = ROWS * blocks - 1
    a, b, e, l, u = factors(alpha, beta, row + ROWS * (lane + me - 1), last)
    weight = (1.0 - 2.0 * alpha + 2.0 * beta) * (1.0 / 16.0)

    def own(x):
        return jnp.broadcast_to(x[:, 1:2], x.shape)

    a_o, b_o, e_o, l_o, u_o, weight_o = [own(x) for x in (a, b, e, l, u, weight)]
    over_e = -1.0 / jnp.where(e_o == 0.0, 1.0, e_o)
    over_a = -1.0 / jnp.where(a_o == 0.0, 1.0, a_o)
    rows_a[0] = b_o * over_e
    rows_a[1] = a_o * over_e
    rows_a[2] = b_o * over_a
    rows_a[3] = e_o * over_a
    one = jnp.ones((1, 128), F32)
    nil = jnp.zeros((1, 128), F32)
    prior, now = nil, one
    prior_d, now_d = nil, one
    rows_a[4, 0:1, :] = now
    rows_a[5, ROWS - 1 : ROWS, :] = nil
    rows_a[5, ROWS - 2 : ROWS - 1, :] = now_d
    for j in range(ROWS - 1):
        prior, now = now, rows_a[0, j : j + 1, :] * now + rows_a[1, j : j + 1, :] * prior
        rows_a[4, j + 1 : j + 2, :] = now
        i = ROWS - 2 - j
        prior_d, now_d = (
            now_d,
            rows_a[2, i : i + 1, :] * now_d + rows_a[3, i : i + 1, :] * prior_d,
        )
        if i > 0:
            rows_a[5, i - 1 : i, :] = now_d
    phi_o = rows_a[4]
    psi_o = rows_a[5]
    sl_o = jnp.where(me == 0, 0.0, psi_o / now_d)
    sr_o = phi_o / now
    wr_o = e_o * (
        phi_o * pltpu.roll(psi_o, ROWS - 1, 0) - pltpu.roll(phi_o, ROWS - 1, 0) * psi_o
    )
    wr_o = 1.0 / jnp.where(row == ROWS - 1, 1.0, wr_o)

    def as_row(x):
        return jnp.sum(jnp.where(row == lane, x, 0.0), axis=0, keepdims=True)

    phi_w = as_row(phi_o * wr_o)
    psi_w = as_row(psi_o * wr_o)
    green = jnp.where(row <= lane, phi_o * psi_w, psi_o * phi_w)
    green = jnp.where((row < ROWS - 1) & (lane < ROWS - 1), green, 0.0)
    a_end, b_end, e_end = a_o[31:32], b_o[31:32], e_o[31:32]
    ratio = jnp.where(e_end == 0.0, 0.0, u_o[31:32] / jnp.where(e_end == 0.0, 1.0, e_end))
    bend = ratio * a_end - l_o[31:32]
    tip = (lane[0:1] == ROWS - 1).astype(F32)
    local = green - l_o * pltpu.roll(green, 1, 0) - u_o * pltpu.roll(green, ROWS - 1, 0)
    end_row = bend * green[30:31] - ratio * tip
    local = jnp.where(row == ROWS - 1, end_row, local)
    pair_row = iota((8, 128), 0)
    pair = jnp.where(
        pair_row == 0,
        tip - a_end * green[30:31],
        jnp.where(pair_row == 1, green[0:1], 0.0),
    )
    shaped = jnp.concatenate([local, pair], axis=0) * as_row(weight_o)
    op = 6.0 * shaped
    op = op - 4.0 * (pltpu.roll(shaped, 1, 1) + pltpu.roll(shaped, 127, 1))
    op = op + (pltpu.roll(shaped, 2, 1) + pltpu.roll(shaped, 126, 1))
    wide = iota((40, 128), 1)
    op = jnp.where(
        wide < 34, op, jnp.where((wide >= 38) & (wide < 40), pltpu.roll(op, 40, 1), 0.0)
    )
    op_high = op.astype(BF16).astype(F32)
    op_low = op - op_high
    packed = jnp.where(wide < 32, op_high, 0.0)
    packed = jnp.where((wide >= 32) & (wide < 64), pltpu.roll(op_high, 32, 1), packed)
    packed = jnp.where((wide >= 64) & (wide < 96), pltpu.roll(op_low, 64, 1), packed)
    packed = jnp.where((wide >= 96) & (wide < 104), pltpu.roll(op_high, 64, 1), packed)
    packed = jnp.where((wide >= 104) & (wide < 112), pltpu.roll(op_high, 72, 1), packed)
    packed = jnp.where((wide >= 112) & (wide < 120), pltpu.roll(op_low, 80, 1), packed)
    wmat[...] = packed.astype(BF16)
    idx = iota((16, 128), 0)
    spread = iota((16, 128), 1)
    field_i = idx - jnp.where(idx >= 5, 5, 0) - jnp.where(idx >= 10, 5, 0)
    kind = jnp.where(idx < 5, op[32:33], jnp.where(idx < 10, op[33:34], 0.0))
    inner = jnp.where(spread < 32, kind, 0.0)
    again = inner + pltpu.roll(inner, 32, 1)
    again = again + pltpu.roll(again, 64, 1)
    place = spread & 31
    place_half = spread & 15
    field_h = place_half >> 1
    ends = [jnp.broadcast_to(kind[:, c : c + 1], (16, 128)) for c in (32, 33, 38, 39)]
    even = (spread & 1) == 0
    outer = jnp.where(
        place < 16, jnp.where(even, ends[0], ends[1]), jnp.where(even, ends[2], ends[3])
    )
    outer = jnp.where(field_h == field_i, outer, 0.0)
    again_high = again.astype(BF16).astype(F32)
    outer_high = outer.astype(BF16).astype(F32)
    quarter = spread >> 5
    for part in range(5):
        lane_at = spread + 128 * part
        field_l = jnp.zeros((16, 128), jnp.int32)
        for q in range(4):
            field_l = jnp.where(quarter == q, (4 * part + q) % 5, field_l)
        own_part = jnp.where(lane_at < 320, again_high, again - again_high)
        own_part = jnp.where(field_l == field_i, own_part, 0.0)
        halo_part = jnp.where(lane_at < 544, outer_high, outer - outer_high)
        value = jnp.where(
            lane_at < 480, own_part, jnp.where(lane_at < 576, halo_part, 0.0)
        )
        wpq[:, 128 * part : 128 * part + 128] = value.astype(BF16)

    sl_before = jnp.where(row == 0, jnp.where(me == 0, 0.0, 1.0), pltpu.roll(sl_o, 1, 0))
    sl_after = jnp.where(row >= ROWS - 2, 0.0, pltpu.roll(sl_o, ROWS - 1, 0))
    sr_before = jnp.where(row == 0, 0.0, pltpu.roll(sr_o, 1, 0))
    sr_after = pltpu.roll(sr_o, ROWS - 1, 0)
    spikes[0] = jnp.where(
        row == ROWS - 1, bend * sl_o[30:31], sl_o - l_o * sl_before - u_o * sl_after
    )
    spikes[1] = jnp.where(
        row == ROWS - 1,
        1.0 + ratio * b_end + bend * sr_o[30:31],
        sr_o - l_o * sr_before - u_o * sr_after,
    )

    tags = [a_end * sl_o[30:31], b_end + a_end * sr_o[30:31], e_end, sl_o[0:1], sr_o[0:1]]
    tag = nil
    for i, value in enumerate(tags):
        tag = jnp.where(lane[0:1] == i, value, tag)

    tag_s[...] = tag


    pl.semaphore_wait(y_sem.at[1], 2)

    def tag_out(step):
        return pltpu.make_async_remote_copy(
            tag_s,
            tags_all.at[me],
            t_send,
            t_recv,
            device_id=(gx, lax.rem(me + 1 + (step + 4) % (blocks - 1), blocks)),
            device_id_type=MESH,
        )

    for step in range(blocks - 1):
        tag_out(step).start()
    pltpu.make_async_copy(tag_s, tags_all.at[me], t_recv).start()

    def pair_out(z, h):
        return pltpu.make_async_remote_copy(
            pqs.at[z, h],
            rbuf.at[me],
            p_send,
            p_recv,
            device_id=(gx, 2 * z + h),
            device_id_type=MESH,
        )

    def pair_own(z, h):
        return pltpu.make_async_copy(pqs.at[z, h], rbuf.at[me], p_recv)

    def messages(step, holds_own):
        pair = [plane_of(2 * step), plane_of(2 * step + 1)]

        @pl.when(me > 0)
        def _():
            for z in pair:
                top_out(z).wait_recv()

        @pl.when(me < blocks - 1)
        def _():
            for z in pair:
                bottom_out(z).wait_recv()

        for z in pair:
            high, low = split(sx[z].reshape(FIELDS * ROWS, COLS))
            blank = jnp.zeros((6, COLS), F32)
            halo_high, halo_low = split(
                jnp.concatenate(
                    [ybot[z, f] for f in range(FIELDS)]
                    + [blank]
                    + [ytop[z, f] for f in range(FIELDS)]
                    + [blank],
                    axis=0,
                )
            )
            stack = jnp.concatenate([high, low, high, halo_high, halo_low, halo_high], axis=0)
            out = jnp.dot(wpq[:, 0:576], stack, preferred_element_type=F32)
            for h in range(2):
                pqs[z, h, 0 : 2 * FIELDS, :] = out[0 : 2 * FIELDS, 128 * h : 128 * h + 128]
        for i, z in enumerate(pair):
            for h in range(2):
                if holds_own and i == 0:

                    @pl.when(2 * z + h == me)
                    def _():
                        pair_own(z, h).start()

                    @pl.when(2 * z + h != me)
                    def _():
                        pair_out(z, h).start()

                else:
                    pair_out(z, h).start()

    @pl.loop(0, planes // 2 - 1)
    def _(step):
        messages(step, False)

    messages(planes // 2 - 1, True)

    pltpu.make_async_copy(tags_all, tags_all, t_recv).wait()

    tagged = jnp.concatenate([tags_all[k] for k in range(blocks)], axis=0)
    block = iota((blocks, 128), 0)

    def quantity(i):
        return jnp.broadcast_to(tagged[:, i : i + 1], (blocks, 128))

    def following(x):
        return jnp.where(block == blocks - 1, 0.0, pltpu.roll(x, blocks - 1, 0))

    e_cut = quantity(2)
    low_c = quantity(0)
    mid_c = quantity(1) + e_cut * following(quantity(3))
    up_c = e_cut * following(quantity(4))
    over_up = -1.0 / jnp.where(up_c == 0.0, 1.0, up_c)
    over_low = -1.0 / jnp.where(low_c == 0.0, 1.0, low_c)
    rows_b[0] = low_c * over_up
    rows_b[1] = mid_c * over_up
    rows_b[2] = mid_c * over_low
    rows_b[3] = up_c * over_low
    rows_b[4, 0:1, :] = one
    rows_b[5, blocks - 1 : blocks, :] = one
    prior, now = nil, one
    prior_d, now_d = nil, one
    for k in range(blocks - 1):
        prior, now = now, rows_b[0, k : k + 1, :] * prior + rows_b[1, k : k + 1, :] * now
        rows_b[4, k + 1 : k + 2, :] = now
        i = blocks - 1 - k
        prior_d, now_d = (
            now_d,
            rows_b[2, i : i + 1, :] * now_d + rows_b[3, i : i + 1, :] * prior_d,
        )
        rows_b[5, i - 1 : i, :] = now_d
    phi_b, psi_b = rows_b[4], rows_b[5]
    leading = jnp.where(block == 0, 0.0, pltpu.roll(phi_b, 1, 0))
    turn = low_c * leading + mid_c * phi_b
    scale = 1.0 / (psi_b * turn + up_c * phi_b * following(psi_b))
    rows_b[6] = phi_b * scale
    rows_b[7] = psi_b * scale
    rows_b[8] = e_cut

    pltpu.make_async_copy(rbuf, rbuf, p_recv).wait()

    right_sides = []
    for k in range(blocks):
        side_k = rbuf[k, 0:FIELDS]
        if k < blocks - 1:
            side_k = side_k - rows_b[8, k : k + 1, :] * rbuf[k + 1, FIELDS : 2 * FIELDS]
        right_sides.append(side_k)
    tail = jnp.zeros((FIELDS, 128), F32)
    for k in range(blocks - 1, -1, -1):
        ss[k + 1] = rows_b[4, k : k + 1, :] * tail
        tail = tail + rows_b[7, k : k + 1, :] * right_sides[k]
    front = jnp.zeros((FIELDS, 128), F32)
    ss[0] = front
    for k in range(blocks):
        front = front + rows_b[6, k : k + 1, :] * right_sides[k]
        ss[k + 1] = ss[k + 1] + rows_b[5, k : k + 1, :] * front

    def sep_out(step):
        k = lax.rem(me + 1 + (step + 4) % (blocks - 1), blocks)
        return pltpu.make_async_remote_copy(
            ss.at[pl.ds(k, 2)],
            sbuf.at[me],
            s_send,
            s_recv,
            device_id=(gx, k),
            device_id_type=MESH,
        )

    for step in range(blocks - 1):
        sep_out(step).start()

    pltpu.make_async_copy(ss.at[pl.ds(me, 2)], sbuf.at[me], s_recv).start()

    @pl.loop(0, planes)
    def _(z):
        weights = wmat[...]
        gap = jnp.zeros((4, COLS), F32)
        for f in range(FIELDS):
            source = sx[z, f]
            high, low = split(source)
            halo = jnp.concatenate([ybot[z, f], gap, ytop[z, f]], axis=0)
            halo_high = halo.astype(BF16).astype(F32)
            halo_low = halo - halo_high
            halos = jnp.concatenate([halo_high, halo_low], axis=0).astype(BF16)
            again = jnp.concatenate([halo_high, jnp.zeros((8, COLS), F32)], axis=0).astype(BF16)
            stack = jnp.concatenate([high, low, high, halos, again], axis=0)
            out = jnp.dot(weights, stack, preferred_element_type=F32)
            zl[z, f] = source - out[0:ROWS]

    @pl.loop(0, planes)
    def _(z):
        @pl.when(me < blocks - 1)
        def _():
            top_out(z).wait_send()

        @pl.when(me > 0)
        def _():
            bottom_out(z).wait_send()

    sent = pl.ds(0, blocks - 1)
    pltpu.make_async_copy(rbuf.at[sent], rbuf.at[sent], p_send).wait()
    pltpu.make_async_copy(tags_all.at[sent], tags_all.at[sent], t_send).wait()
    pltpu.make_async_copy(sbuf, sbuf, s_recv).wait()
    pltpu.make_async_copy(sbuf.at[sent], sbuf.at[sent], s_send).wait()


def finish(planes, zl, nin, sbuf, spikes, new_state, new_inc, ready, state_sem, inc_sem):
    def inc_out(z):
        return pltpu.make_async_copy(nin.at[z], new_inc.at[:, z], inc_sem.at[z])

    def state_out(z):
        return pltpu.make_async_copy(ready.at[z], new_state.at[:, z], state_sem.at[z])

    @pl.loop(0, planes)
    def _(z):
        for h in range(2):
            k = 2 * z + h
            cols = slice(128 * h, 128 * h + 128)
            for f in range(FIELDS):
                under = sbuf[k, 0, f : f + 1, :]
                over = sbuf[k, 1, f : f + 1, :]
                ready[z, f, :, cols] = (
                    zl[z, f, :, cols] - spikes[0] * under - spikes[1] * over
                )
        state_out(z).start()
        inc_out(z).start()

    @pl.loop(0, planes)
    def _(z):
        state_out(z).wait()
        inc_out(z).wait()


def shards(state, increment, jacobian, filter_alpha, filter_beta):
    fields, planes, rows, cols = state.shape
    blocks = lax.axis_size("gy")
    widths = lax.axis_size("gx")
    groups = planes // 4
    full = (planes, fields, rows, cols)
    halo = (planes, fields, 2, cols)
    dma = pltpu.SemaphoreType.DMA
    anywhere = pl.BlockSpec(memory_space=pltpu.HBM)
    near = pl.BlockSpec(memory_space=pltpu.VMEM)
    whole = jax.ShapeDtypeStruct(state.shape, F32)
    zl, nin, sbuf, spikes = pl.pallas_call(
        functools.partial(kernel, blocks, planes, widths),
        out_shape=(
            jax.ShapeDtypeStruct(full, F32),
            jax.ShapeDtypeStruct(full, F32),
            jax.ShapeDtypeStruct((blocks, 2, fields, 128), F32),
            jax.ShapeDtypeStruct((2, rows, 128), F32),
        ),
        in_specs=[anywhere] * 6,
        out_specs=(near,) * 4,
        scratch_shapes=[
            pltpu.VMEM(full, F32),
            pltpu.VMEM(full, F32),
            pltpu.VMEM(full, F32),
            pltpu.VMEM(full, F32),
            pltpu.VMEM((fields * fields, rows, 128), F32),
            pltpu.VMEM((fields, fields, rows), F32),
            pltpu.VMEM((cols, cols), BF16),
            pltpu.VMEM((groups, rows, 128), F32),
            pltpu.VMEM(((groups + 1) // 2, rows, 128), F32),
            pltpu.VMEM(((groups + 1) // 2, rows, 128), F32),
            pltpu.VMEM(((groups + 1) // 2, rows, 128), F32),
            pltpu.VMEM(((groups + 1) // 2, rows, 128), F32),
            pltpu.VMEM(halo, F32),
            pltpu.VMEM(halo, F32),
            pltpu.VMEM(halo, F32),
            pltpu.VMEM(halo, F32),
            pltpu.VMEM((2, 1, rows), F32),
            pltpu.VMEM((1, 128), F32),
            pltpu.VMEM((2, 1, 128), F32),
            pltpu.VMEM((128, 128), F32),
            pltpu.VMEM((6, rows, 128), F32),
            pltpu.VMEM((9, blocks, 128), F32),
            pltpu.VMEM((16, 640), BF16),
            pltpu.VMEM((1, 128), F32),
            pltpu.VMEM((blocks, 1, 128), F32),
            pltpu.VMEM((planes, 2, MESSAGE, 128), F32),
            pltpu.VMEM((blocks, MESSAGE, 128), F32),
            pltpu.VMEM((blocks + 1, fields, 128), F32),
            pltpu.VMEM((40, 128), BF16),
            dma((planes,)),
            dma((planes,)),
            dma((4,)),
            pltpu.SemaphoreType.REGULAR((3,)),
            pltpu.SemaphoreType.REGULAR((2,)),
            dma((2,)),
            dma((2,)),
            dma((2,)),
            dma((2,)),
            dma((planes,)),
            dma((planes,)),
            dma((planes,)),
            dma((planes,)),
            dma,
            dma,
            dma,
            dma,
            dma,
            dma,
        ],
        compiler_params=pltpu.CompilerParams(
            collective_id=0, has_side_effects=True, vmem_limit_bytes=32 * 1024 * 1024
        ),
    )(
        *[
            pltpu.with_memory_space_constraint(x, pltpu.HBM)
            for x in (
                state,
                increment,
                filter_alpha.reshape(1, rows),
                filter_beta.reshape(1, rows),
                jacobian,
                stencil_weights(),
            )
        ]
    )
    return pl.pallas_call(
        functools.partial(finish, planes),
        out_shape=(whole, whole),
        in_specs=[near] * 4,
        out_specs=(anywhere, anywhere),
        scratch_shapes=[pltpu.VMEM(full, F32), dma((planes,)), dma((planes,))],
        compiler_params=pltpu.CompilerParams(vmem_limit_bytes=24 * 1024 * 1024),
    )(zl, nin, sbuf, spikes)


def solution(mesh):
    placed = (
        P(None, None, "gy", "gx"),
        P(None, None, "gy", "gx"),
        P(None, None, "gy"),
        P("gy"),
        P("gy"),
    )
    return jax.shard_map(
        shards,
        mesh=mesh,
        in_specs=placed,
        out_specs=(P(None, None, "gy", "gx"), P(None, None, "gy", "gx")),
        check_vma=False,
    )
```
